32 devices in a mesh: fsdp: 2 (over y), ctx: 4 (over z), tp: 4 (over x, core).
Axes of the slice: x: 2, y: 2, z: 4, core: 2. Of those that a mesh axis runs over, the one named last changes fastest.
Arguments:
- tokens: bfloat16 [4096, 2048], P(('fsdp', 'ctx')), may hold values from -6 to 6
- token_segment: int32 [4096], P('fsdp'), may hold values from 0 to 12, as said below
- segment_parent: int32 [2, 13], P('fsdp'), may hold values from 0 to 4, as said below
- ln1_gain: bfloat16 [2048], replicated, may hold values from 0.5 to 1.5
- ln1_bias: bfloat16 [2048], replicated, may hold values from -1.1953125 to 1.1953125
- q_weight: bfloat16 [2048, 2048], P(('fsdp', 'ctx'), 'tp'), may hold values from -0.125 to 0.125
- q_bias: bfloat16 [2048], P('tp'), may hold values from -1.1953125 to 1.1953125
- kv_weight: bfloat16 [2048, 256], P(('fsdp', 'ctx')), may hold values from -0.125 to 0.125
- value_bias: bfloat16 [128], replicated, may hold values from -1.1953125 to 1.1953125
- o_weight: bfloat16 [2048, 2048], P('tp', ('fsdp', 'ctx')), may hold values from -1.5 to 1.5
- o_bias: bfloat16 [2048], replicated, may hold values from -1.1953125 to 1.1953125
- ln2_gain: bfloat16 [2048], replicated, may hold values from 0.5 to 1.5
- ln2_bias: bfloat16 [2048], replicated, may hold values from -1.1953125 to 1.1953125
- up_weight: bfloat16 [2048, 8192], P(('fsdp', 'ctx'), 'tp'), may hold values from -0.125 to 0.125
- up_bias: bfloat16 [8192], P('tp'), may hold values from -1.1953125 to 1.1953125
- down_weight: bfloat16 [8192, 2048], P('tp', ('fsdp', 'ctx')), may hold values from -0.0625 to 0.0625
- down_bias: bfloat16 [2048], replicated, may hold values from -1.1953125 to 1.1953125
- out_grad: bfloat16 [4096, 2048], P(('fsdp', 'ctx')), may hold values from -6 to 6
Outputs:
- layer_out: bfloat16 [4096, 2048], P(('fsdp', 'ctx', 'tp'))
- input_grad: bfloat16 [4096, 2048], P(('fsdp', 'ctx', 'tp'))
- ln1_gain_grad: float32 [2048], replicated
- ln1_bias_grad: float32 [2048], replicated
- q_weight_grad: float32 [2048, 2048], P(('fsdp', 'ctx'), 'tp')
- q_bias_grad: float32 [2048], P('tp')
- kv_weight_grad: float32 [2048, 256], P(('fsdp', 'ctx', 'tp'))
- value_bias_grad: float32 [128], replicated
- o_weight_grad: float32 [2048, 2048], P('tp', ('fsdp', 'ctx'))
- o_bias_grad: float32 [2048], replicated
- ln2_gain_grad: float32 [2048], replicated
- ln2_bias_grad: float32 [2048], replicated
- up_weight_grad: float32 [2048, 8192], P(('fsdp', 'ctx'), 'tp')
- up_bias_grad: float32 [8192], P('tp')
- down_weight_grad: float32 [8192, 2048], P('tp', ('fsdp', 'ctx'))
- down_bias_grad: float32 [2048], replicated
The draws below stay inside these ranges and needn't reach their ends.
Inputs may be any that keep to these rules, and one draw needn't show every extreme that they name: `segment_parent`: row t gives the parent of each of the 13 segments of tree t: segment 0 is the trunk and its own parent, segments 1 to 4 are branches with parent 0, every later segment is a leaf whose parent is a branch, and each branch has 2 leaves. `token_segment`: within each tree the segment ids never fall, the first 768 tokens are segment 0, and every segment has at least one token.
All inputs are finite; a program needn't handle non-finite values.
Results may differ from the reference program's by a relative error of at most 0.02.
Values may be sent and summed in bfloat16 or wider, within the bound.
No kernel may reach another device: no remote copies, remote signals or barrier semaphores. Data moves between devices by JAX's collectives and lax.ppermute only.
A program may use at most 192 MiB of HBM per device.

```python
import math
import jax
import jax.numpy as jnp
from jax import lax

D = 2048
HEADS = 16
HEAD_DIM = 128
FF = 8192
BRANCHES = 4
LEAVES = 2
TREES = 2
TREE_LEN = 2048
TRUNK = 768
SEGS = 13
TOKENS = 4096


def tree_layout(key, tree_index):
    tree_key = jax.random.fold_in(jax.random.fold_in(key, 911), tree_index)
    leaf_key, cut_key = jax.random.split(tree_key)
    owners = jnp.repeat(jnp.arange(1, BRANCHES + 1, dtype=jnp.int32), LEAVES)
    owners = jax.random.permutation(leaf_key, owners)
    parent = jnp.concatenate([jnp.zeros((1 + BRANCHES,), jnp.int32), owners])
    others = SEGS - 1
    rest_len = TREE_LEN - TRUNK
    least_len = rest_len // (2 * others)
    spare_rest = rest_len - others * least_len
    cut_points = jnp.sort(jax.random.randint(cut_key, (others - 1,), 0, spare_rest + 1, dtype=jnp.int32))
    bounds = jnp.concatenate([jnp.zeros((1,), jnp.int32), cut_points, jnp.full((1,), spare_rest, jnp.int32)])
    lengths = least_len + (bounds[1:] - bounds[:-1])
    starts = TRUNK + jnp.cumsum(lengths) - lengths
    positions = jnp.arange(TREE_LEN, dtype=jnp.int32)
    segment = jnp.sum((positions[:, None] >= starts[None, :]).astype(jnp.int32), axis=1)
    return (parent, segment.astype(jnp.int32))


def draw_token_segment(key, part):
    layouts = jax.vmap(lambda tree_index: tree_layout(key, tree_index)[1])(jnp.arange(TREES, dtype=jnp.int32))
    return layouts.reshape(TREES * TREE_LEN)


def draw_segment_parent(key, part):
    return jax.vmap(lambda tree_index: tree_layout(key, tree_index)[0])(jnp.arange(TREES, dtype=jnp.int32))


def spiked(drawn, rng, source, target, shards_of, factor):
    owner, partner = [(jnp.arange(drawn.shape[position]) // (drawn.shape[position] // shards_of)).reshape([-1 if axis == position else 1 for axis in range(drawn.ndim)]) for position in (source, target)]
    chosen = jax.random.permutation(rng, shards_of)[partner]
    strong = (owner == chosen) | (owner == (partner + shards_of // 2) % shards_of)
    return jnp.where(strong, factor * drawn, drawn)


def shard_levels(key, shape, cuts, low, top_value):
    loudness, own = 1.0, jax.random.fold_in(key, 6)
    for dim, parts in cuts:
        draws = jnp.exp(jax.random.uniform(jax.random.fold_in(own, dim), (parts,), jnp.float32, low / len(cuts), top_value / len(cuts)))
        loudness = loudness * jnp.repeat(draws, shape[dim] // parts).reshape([-1 if axis == dim else 1 for axis in range(len(shape))])
    return loudness


def normal_values(rng, extent, scale, limit, shards=(), kind=jnp.bfloat16):
    result = scale * jax.random.normal(rng, extent, jnp.float32)
    if shards:
        result = result * shard_levels(rng, extent, shards, -0.22, 0.18)
    return jnp.clip(result, -limit, limit).astype(kind)


def gaussian_with(rng, dims, scale, bound, cuts, heavy, kind=jnp.bfloat16):
    result = scale * jax.random.normal(rng, dims, jnp.float32)
    if cuts:
        result = result * shard_levels(rng, dims, cuts, -0.22, 0.18)
    return jnp.clip(spiked(result, jax.random.fold_in(rng, 3), *heavy), -bound, bound).astype(kind)


def setup_inputs(seed: int = 0) -> dict:
    splits = jax.random.split(jax.random.key(seed), 19)
    return {
        "tokens": gaussian_with(splits[0], (TOKENS, D), 1.0, 6.0, ((0, 8),), (0, 1, 8, 2.0)),
        "token_segment": draw_token_segment(jax.random.fold_in(splits[18], 71), 0),
        "segment_parent": draw_segment_parent(jax.random.fold_in(splits[18], 71), 0),
        "ln1_gain": jnp.clip(1.0 + 0.1 * jax.random.normal(splits[3], (D,), jnp.float32), 0.5, 1.5).astype(jnp.bfloat16),
        "ln1_bias": normal_values(splits[4], (D,), 0.2, 1.1953125),
        "q_weight": normal_values(splits[5], (D, HEADS * HEAD_DIM), D ** -0.5, 0.125, ((0, 8), (1, 4))),
        "q_bias": normal_values(splits[6], (HEADS * HEAD_DIM,), 0.2, 1.1953125, ((0, 4),)),
        "kv_weight": normal_values(splits[7], (D, 2 * HEAD_DIM), D ** -0.5, 0.125, ((0, 8),)),
        "value_bias": normal_values(splits[8], (HEAD_DIM,), 0.2, 1.1953125),
        "o_weight": normal_values(splits[9], (HEADS * HEAD_DIM, D), (max(HEADS * HEAD_DIM // 128, 1)) ** -0.5, 1.5, ((0, 4), (1, 8))),
        "o_bias": normal_values(splits[10], (D,), 0.2, 1.1953125),
        "ln2_gain": jnp.clip(1.0 + 0.1 * jax.random.normal(splits[11], (D,), jnp.float32), 0.5, 1.5).astype(jnp.bfloat16),
        "ln2_bias": normal_values(splits[12], (D,), 0.2, 1.1953125),
        "up_weight": normal_values(splits[13], (D, FF), D ** -0.5, 0.125, ((0, 8), (1, 4))),
        "up_bias": normal_values(splits[14], (FF,), 0.2, 1.1953125, ((0, 4),)),
        "down_weight": normal_values(splits[15], (FF, D), FF ** -0.5, 0.0625, ((0, 4), (1, 8))),
        "down_bias": normal_values(splits[16], (D,), 0.2, 1.1953125),
        "out_grad": gaussian_with(splits[17], (TOKENS, D), 1.0, 6.0, ((0, 8),), (0, 1, 8, 2.0)),
    }


@jax.custom_vjp
def low(v):
    return lax.optimization_barrier(v.astype(jnp.bfloat16)).astype(jnp.float32)

@jax.custom_vjp
def low_back(v):
    return v

def low_keep(v):
    return (low(v), None)

def low_pass(kept, grad):
    return (grad,)

def back_keep(v):
    return (v, None)

def back_low(kept, grad):
    return (low(grad),)
low.defvjp(low_keep, low_pass)
low_back.defvjp(back_keep, back_low)
eps = 1e-05
masked_score = -1000000000.0
highest = lax.Precision.HIGHEST

def layer_norm(values, gain, shift):
    center = lax.optimization_barrier(jnp.mean(values, axis=-1, keepdims=True))
    centred = values - center
    spread = lax.optimization_barrier(jnp.mean(centred * centred, axis=-1, keepdims=True))
    return centred * lax.rsqrt(spread + eps) * gain + shift

def matmul(left, right):
    return jnp.dot(left, right, precision=highest, preferred_element_type=jnp.float32)

def tree_forward(params, tree_tokens, tree_segments, parents):
    gain_one, shift_one, query_w, query_b, kv_w, value_b, out_w, out_b, gain_two, shift_two, up_w, up_b, down_w, down_b = params
    score_scale = 1.0 / math.sqrt(HEAD_DIM)
    act_one = low(layer_norm(tree_tokens, gain_one, shift_one))
    queries = low(low_back(matmul(act_one, query_w) + query_b))
    kv_shift = jnp.concatenate([jnp.zeros_like(value_b), value_b])
    kv_rows = low(low_back(matmul(act_one, kv_w) + kv_shift))
    keys_all = kv_rows[:, :HEAD_DIM]
    values_all = kv_rows[:, HEAD_DIM:]
    one_up = parents[tree_segments].astype(jnp.int32)
    two_up = parents[one_up].astype(jnp.int32)
    places = jnp.arange(TREE_LEN, dtype=jnp.int32)
    block_rows = min(512, TREE_LEN)
    block_count = TREE_LEN // block_rows

    def attend(inputs):
        query_block, own_seg, seg_one, seg_two, query_place = inputs
        raw_scores = jnp.einsum('qhd,kd->hqk', query_block, keys_all, precision=highest, preferred_element_type=jnp.float32) * score_scale
        same_path = (tree_segments[None, :] == own_seg[:, None]) | (tree_segments[None, :] == seg_one[:, None]) | (tree_segments[None, :] == seg_two[:, None])
        allowed = same_path & (places[None, :] <= query_place[:, None])
        scores = low_back(jnp.where(allowed[None, :, :], raw_scores, masked_score))
        row_max = lax.optimization_barrier(jnp.max(scores, axis=2, keepdims=True))
        exp_scores = jnp.exp(scores - row_max)
        attn_probs = low(exp_scores / lax.optimization_barrier(jnp.sum(exp_scores, axis=2, keepdims=True)))
        mixed_rows = jnp.einsum('hqk,kd->qhd', attn_probs, values_all, precision=highest, preferred_element_type=jnp.float32)
        return mixed_rows.reshape(block_rows, HEADS * HEAD_DIM)
    mixed_blocks = lax.map(jax.checkpoint(attend), (queries.reshape(block_count, block_rows, HEADS, HEAD_DIM), tree_segments.reshape(block_count, block_rows), one_up.reshape(block_count, block_rows), two_up.reshape(block_count, block_rows), places.reshape(block_count, block_rows)))
    attended = low(low_back(mixed_blocks.reshape(TREE_LEN, HEADS * HEAD_DIM)))
    residual = tree_tokens + low_back(matmul(attended, out_w) + out_b)
    act_two = low(layer_norm(residual, gain_two, shift_two))
    pre_act = low_back(matmul(act_two, up_w) + up_b)
    hidden = low(jax.nn.gelu(pre_act, approximate=True))
    return residual + low_back(matmul(hidden, down_w) + down_b)

def reference(tokens, token_segment, segment_parent, ln1_gain, ln1_bias, q_weight, q_bias, kv_weight, value_bias, o_weight, o_bias, ln2_gain, ln2_bias, up_weight, up_bias, down_weight, down_bias, out_grad):
    params = tuple((weight_arr.astype(jnp.float32) for weight_arr in (ln1_gain, ln1_bias, q_weight, q_bias, kv_weight, value_bias, o_weight, o_bias, ln2_gain, ln2_bias, up_weight, up_bias, down_weight, down_bias)))
    tree_inputs = tokens.astype(jnp.float32).reshape(TREES, TREE_LEN, D)
    tree_cotangents = out_grad.astype(jnp.float32).reshape(TREES, TREE_LEN, D)
    tree_segs = token_segment.reshape(TREES, TREE_LEN)

    def one_tree(totals, inputs):
        tree_tokens, tree_cotangent, tree_segments, parents = inputs

        def forward(weights_in, tokens_in):
            return tree_forward(weights_in, tokens_in, tree_segments, parents)
        tree_out, pullback = jax.vjp(forward, params, tree_tokens)
        weight_grads, token_grads = pullback(tree_cotangent)
        totals = jax.tree.map(jnp.add, totals, weight_grads)
        return (totals, (tree_out.astype(jnp.bfloat16), token_grads.astype(jnp.bfloat16)))
    start_totals = jax.tree.map(jnp.zeros_like, params)
    totals, (tree_outs, tree_dx) = lax.scan(one_tree, start_totals, (tree_inputs, tree_cotangents, tree_segs, segment_parent))
    layer_out = tree_outs.reshape(TOKENS, D)
    input_grad = tree_dx.reshape(TOKENS, D)
    return (layer_out, input_grad, totals[0], totals[1], totals[2], totals[3], totals[4], totals[5], totals[6], totals[7], totals[8], totals[9], totals[10], totals[11], totals[12], totals[13])
```

```python
import math

import jax
import jax.numpy as jnp
import numpy as np
from jax import lax
from jax.sharding import PartitionSpec as P

eps = 1e-05
masked_score = -1000000000.0
f32 = jnp.float32
bf16 = jnp.bfloat16
ring_axes = ("fsdp", "ctx")


def ring_order(rows, cols):
    if rows == 1:
        return list(range(cols))
    if cols == 1:
        return list(range(rows))
    if rows % 2 == 0:
        walk = [(0, c) for c in range(cols)]
        for step, c in enumerate(range(cols - 1, -1, -1)):
            span = range(1, rows) if step % 2 == 0 else range(rows - 1, 0, -1)
            walk += [(r, c) for r in span]
        if cols % 2 == 0 or rows == 2:
            return [r * cols + c for r, c in walk]
    return list(range(rows * cols))


class Ring:
    def __init__(self, rows, cols, place):
        self.size = rows * cols
        order = ring_order(rows, cols)
        where = [0] * self.size
        for spot, owner in enumerate(order):
            where[owner] = spot
        n = self.size
        self.right = [(order[i], order[(i + 1) % n]) for i in range(n)]
        self.left = [(b, a) for a, b in self.right]
        spot = jnp.asarray(np.array(where, np.int32))[place]
        self.slots = jnp.asarray(np.array(order, np.int32))[
            lax.rem(spot - jnp.arange(n, dtype=jnp.int32) + n, n)
        ]
        self.homes = lax.rem(spot - jnp.asarray(np.array(where, np.int32)) + n, n)

    def hops(self, flip):
        far = self.size // 2
        near = self.size - 1 - far
        return (near, far) if flip else (far, near)

    def gather(self, shard, flip):
        hops_right, hops_left = self.hops(flip)
        slots = [shard] * self.size
        moving = shard
        for k in range(1, hops_right + 1):
            moving = lax.ppermute(moving, ring_axes, self.right)
            slots[k] = moving
        moving = shard
        for k in range(1, hops_left + 1):
            moving = lax.ppermute(moving, ring_axes, self.left)
            slots[self.size - k] = moving
        return slots

    def scatter(self, part, flip):
        hops_right, hops_left = self.hops(flip)
        n = self.size
        total = part(0)
        for hops, sign, pairs in ((hops_right, -1, self.right), (hops_left, 1, self.left)):
            moving = None
            for k in range(hops, 0, -1):
                piece = part((sign * k) % n)
                if moving is not None:
                    piece = piece + moving.astype(f32)
                moving = lax.ppermute(piece.astype(bf16), ring_axes, pairs)
            if moving is not None:
                total = total + moving.astype(f32)
        return total

    def into(self, values):
        width = values.shape[-1] // self.size
        return jnp.concatenate(
            [
                lax.dynamic_slice_in_dim(values, self.slots[k] * width, width, values.ndim - 1)
                for k in range(self.size)
            ],
            axis=-1,
        )

    def back(self, values):
        width = values.shape[-1] // self.size
        return jnp.concatenate(
            [
                lax.dynamic_slice_in_dim(values, self.homes[k] * width, width, values.ndim - 1)
                for k in range(self.size)
            ],
            axis=-1,
        )


def swap(values, axis, bit):
    count = lax.axis_size(axis)
    return lax.ppermute(values, axis, [(i, i ^ bit) for i in range(count)])


def bits_of(axis):
    count = lax.axis_size(axis)
    bit = 1
    while bit < count:
        yield bit
        bit *= 2


def share_sum(rows):
    for bit in bits_of("tp"):
        count = lax.axis_size("tp") // bit
        pairs = rows.reshape((count // 2, 2) + (-1,) + rows.shape[1:])
        other = swap(pairs[:, 1].astype(bf16), "tp", bit)
        rows = pairs[:, 0].astype(f32) + other.astype(f32)
        rows = rows.reshape((-1,) + rows.shape[2:])
    return rows


def share_spread(rows):
    for bit in reversed(list(bits_of("tp"))):
        rows = rows.reshape((-1, 1) + (lax.axis_size("tp") and rows.shape[-2:]))
        rows = jnp.concatenate([rows, swap(rows, "tp", bit)], axis=1)
        rows = rows.reshape((-1,) + rows.shape[2:])
    return rows.reshape((-1,) + rows.shape[-1:])


def everyone_sum(values, axes):
    for axis in axes:
        for bit in bits_of(axis):
            values = values + swap(values, axis, bit)
    return values


def dot(left, right, dims):
    return lax.dot_general(left, right, (dims, ((), ())), preferred_element_type=f32)


NN = ((1,), (0,))
NT = ((1,), (1,))
TN = ((0,), (0,))


def normed(values):
    center = jnp.mean(values, axis=-1, keepdims=True)
    centred = values - center
    spread = jnp.mean(centred * centred, axis=-1, keepdims=True)
    inv = lax.rsqrt(spread + eps)
    return centred * inv, inv


def normed_back(grad, gain, norm, inv):
    pulled = grad * gain
    term = pulled - jnp.mean(pulled, axis=-1, keepdims=True)
    return inv * (term - norm * jnp.mean(pulled * norm, axis=-1, keepdims=True))


def parent_lookup(seg_ids, parents):
    labels = jnp.arange(parents.shape[0], dtype=jnp.int32)
    picked = jnp.where(seg_ids[:, None] == labels[None, :], parents[None, :], 0)
    return jnp.sum(picked, axis=1)


def gelu_parts(values):
    scale = math.sqrt(2.0 / math.pi)
    squared = values * values
    bend = jnp.tanh(scale * (values + 0.044715 * squared * values))
    out = 0.5 * values * (1.0 + bend)
    slope = 0.5 * (1.0 + bend) + 0.5 * values * (1.0 - bend * bend) * scale * (
        1.0 + 3 * 0.044715 * squared
    )
    return out, slope


def body(
    tokens,
    token_segment,
    segment_parent,
    ln1_gain,
    ln1_bias,
    q_weight,
    q_bias,
    kv_weight,
    value_bias,
    o_weight,
    o_bias,
    ln2_gain,
    ln2_bias,
    up_weight,
    up_bias,
    down_weight,
    down_bias,
    out_grad,
):
    row_count, width = tokens.shape
    head_size = value_bias.shape[0]
    local_width = q_weight.shape[1]
    local_heads = local_width // head_size
    tree_length = token_segment.shape[0]
    score_scale = 1.0 / math.sqrt(head_size)
    ctx_count = lax.axis_size("ctx")
    tp_count = lax.axis_size("tp")
    ctx_index = lax.axis_index("ctx")
    tp_index = lax.axis_index("tp")
    share_rows = row_count // tp_count
    ring = Ring(lax.axis_size("fsdp"), ctx_count, lax.axis_index("fsdp") * ctx_count + ctx_index)
    n = ring.size
    piece = width // n

    qkv_slots = ring.gather(jnp.concatenate([q_weight, kv_weight], axis=1), False)
    o_slots = ring.gather(o_weight, True)
    up_slots = ring.gather(up_weight, False)
    down_slots = ring.gather(down_weight, True)

    row_blocks = [tp_index ^ j for j in range(tp_count)]

    def rows_in(values):
        return jnp.concatenate(
            [
                lax.dynamic_slice_in_dim(values, b * share_rows, share_rows, 0)
                for b in row_blocks
            ],
            axis=0,
        )

    x_low = ring.into(rows_in(tokens))
    g_low = ring.into(rows_in(out_grad))
    vectors = ring.into(
        jnp.stack([ln1_gain, ln1_bias, o_bias, ln2_gain, ln2_bias, down_bias])
    ).astype(f32)
    gain_one, shift_one, o_shift, gain_two, shift_two, down_shift = (
        vectors[i : i + 1] for i in range(6)
    )
    own_place = rows_in(jnp.arange(row_count, dtype=jnp.int32))

    parents = segment_parent[0]
    query_place = ctx_index * row_count + own_place
    key_places = []
    for d in range(ctx_count):
        start = (ctx_index - d) * row_count
        key_places.append(jnp.where(start >= 0, start + own_place, tree_length))
    key_place = jnp.concatenate(key_places)
    segment_blocks = rows_in(token_segment.reshape(ctx_count, row_count).T)
    own_seg = lax.dynamic_slice_in_dim(segment_blocks, ctx_index, 1, 1)[:, 0]
    key_segment = jnp.concatenate(
        [
            lax.dynamic_slice_in_dim(
                segment_blocks, lax.rem(ctx_index - d + ctx_count, ctx_count), 1, 1
            )[:, 0]
            for d in range(ctx_count)
        ]
    )
    seg_one = parent_lookup(own_seg, parents)
    seg_two = parent_lookup(seg_one, parents)
    allowed = (
        (key_segment[None, :] == own_seg[:, None])
        | (key_segment[None, :] == seg_one[:, None])
        | (key_segment[None, :] == seg_two[:, None])
    ) & (key_place[None, :] <= query_place[:, None])

    norm_one, inv_one = normed(x_low.astype(f32))
    act_one = (norm_one * gain_one + shift_one).astype(bf16)
    qkv_full = jnp.concatenate(qkv_slots, axis=0)
    qkv_shift = jnp.concatenate(
        [q_bias.astype(f32), jnp.zeros((head_size,), f32), value_bias.astype(f32)]
    )
    qkv = (dot(act_one, qkv_full, NN) + qkv_shift).astype(bf16)
    queries = qkv[:, :local_width]
    kv_own = qkv[:, local_width:]
    kv_rows = jnp.concatenate(
        [kv_own]
        + [
            lax.ppermute(kv_own, "ctx", [(c, c + d) for c in range(ctx_count - d)])
            for d in range(1, ctx_count)
        ],
        axis=0,
    )
    keys_all = kv_rows[:, :head_size]
    values_all = kv_rows[:, head_size:]

    def scores_of(h):
        raw = dot(queries[:, h * head_size : (h + 1) * head_size], keys_all, NT) * score_scale
        return jnp.where(allowed, raw, masked_score)

    mixed, logs = [], []
    for h in range(local_heads):
        scores = scores_of(h)
        row_max = jnp.max(scores, axis=1, keepdims=True)
        exp_scores = jnp.exp(scores - row_max)
        row_total = jnp.sum(exp_scores, axis=1, keepdims=True)
        probs_low = (exp_scores / row_total).astype(bf16)
        mixed.append(dot(probs_low, values_all, NN).astype(bf16))
        logs.append(row_max + jnp.log(row_total))
    attended = jnp.concatenate(mixed, axis=1)

    o_full = jnp.concatenate(o_slots, axis=1)
    attn_share = share_sum(dot(attended, o_full, NN).astype(bf16))
    x_share = x_low[:share_rows].astype(f32)
    residual = x_share + (attn_share + o_shift)
    norm_two, inv_two = normed(residual)
    act_two = share_spread((norm_two * gain_two + shift_two).astype(bf16))

    up_full = jnp.concatenate(up_slots, axis=0)
    pre_act = dot(act_two, up_full, NN) + up_bias.astype(f32)
    gelu_out, gelu_slope = gelu_parts(pre_act)
    hidden = gelu_out.astype(bf16)
    down_w_grad = ring.scatter(
        lambda k: dot(hidden, g_low[:, k * piece : (k + 1) * piece], TN), False
    )
    down_full = jnp.concatenate(down_slots, axis=1)
    grad_hidden = dot(g_low, down_full, NT)
    grad_pre = (grad_hidden * gelu_slope).astype(bf16)
    up_w_grad = ring.scatter(
        lambda k: dot(act_two[:, k * piece : (k + 1) * piece], grad_pre, TN), True
    )
    grad_two = share_sum(dot(grad_pre, up_full, NT).astype(bf16))
    ffn_share = share_sum(dot(hidden, down_full, NN).astype(bf16))
    layer_out = ring.back((residual + (ffn_share + down_shift)).astype(bf16))

    up_bias_grad = jnp.sum(grad_pre.astype(f32), axis=0)
    g_share = g_low[:share_rows].astype(f32)
    grad_res = g_share + normed_back(grad_two, gain_two, norm_two, inv_two)
    grad_attn_share = grad_res.astype(bf16)
    grad_attn = share_spread(grad_attn_share)
    out_w_grad = ring.scatter(
        lambda k: dot(attended, grad_attn[:, k * piece : (k + 1) * piece], TN), False
    )
    grad_attended = dot(grad_attn, o_full, NT).astype(bf16)
    early = jnp.stack(
        [
            jnp.sum(g_share, axis=0),
            jnp.sum(grad_attn_share.astype(f32), axis=0),
            jnp.sum(grad_two * norm_two, axis=0),
            jnp.sum(grad_two, axis=0),
        ]
    )
    early = everyone_sum(ring.back(early), ("tp", "ctx", "fsdp"))
    up_bias_out = everyone_sum(up_bias_grad, ("ctx", "fsdp"))

    key_grad = jnp.zeros((tree_length, head_size), f32)
    value_grad = jnp.zeros((tree_length, head_size), f32)
    query_grads = []
    for h in range(local_heads):
        cols = slice(h * head_size, (h + 1) * head_size)
        attn_probs = jnp.exp(scores_of(h) - logs[h])
        probs_low = attn_probs.astype(bf16)
        grad_head = grad_attended[:, cols]
        grad_probs = dot(grad_head, values_all, NT)
        row_delta = jnp.sum(attn_probs * grad_probs, axis=1, keepdims=True)
        grad_scores = (attn_probs * (grad_probs - row_delta)).astype(bf16)
        query_grads.append((dot(grad_scores, keys_all, NN) * score_scale).astype(bf16))
        key_grad = key_grad + dot(grad_scores, queries[:, cols], TN) * score_scale
        value_grad = value_grad + dot(probs_low, grad_head, TN)
    grad_query = jnp.concatenate(query_grads, axis=1)
    q_bias_grad = jnp.sum(grad_query.astype(f32), axis=0)

    kv_part = jnp.concatenate([key_grad, value_grad], axis=1).astype(bf16)
    kv_part = kv_part.reshape(ctx_count, tp_count, share_rows, 2 * head_size)
    kv_part = jnp.swapaxes(kv_part, 0, 1).reshape(tp_count * ctx_count * share_rows, -1)
    kv_part = share_sum(kv_part).reshape(ctx_count, share_rows, 2 * head_size)
    kv_sum = kv_part[0]
    for d in range(1, ctx_count):
        kv_sum = kv_sum + lax.ppermute(
            kv_part[d].astype(bf16), "ctx", [(c, c - d) for c in range(d, ctx_count)]
        ).astype(f32)
    kv_low_share = kv_sum.astype(bf16)
    kv_low = share_spread(kv_low_share)

    sub = piece // tp_count
    kv_cols = act_one.reshape(row_count, n, tp_count, sub)
    kv_cols = lax.dynamic_slice_in_dim(kv_cols, tp_index, 1, 2).reshape(row_count, n * sub)

    def q_kv_part(k):
        q_piece = dot(act_one[:, k * piece : (k + 1) * piece], grad_query, TN)
        kv_piece = dot(kv_cols[:, k * sub : (k + 1) * sub], kv_low, TN)
        return jnp.concatenate([q_piece.reshape(-1), kv_piece.reshape(-1)]).reshape(
            -1, local_width
        )

    q_kv = ring.scatter(q_kv_part, True)
    q_w_grad = q_kv[:piece]
    kv_w_grad = q_kv[piece:].reshape(sub, 2 * head_size)

    q_full = qkv_full[:, :local_width]
    kv_full = qkv_full[:, local_width:]
    grad_act = share_sum(dot(grad_query, q_full, NT).astype(bf16)) + dot(
        kv_low_share, kv_full, NT
    )
    norm_share = norm_one[:share_rows]
    inv_share = inv_one[:share_rows]
    input_grad = ring.back(
        (grad_res + normed_back(grad_act, gain_one, norm_share, inv_share)).astype(bf16)
    )
    late = jnp.stack([jnp.sum(grad_act * norm_share, axis=0), jnp.sum(grad_act, axis=0)])
    late = ring.back(late).reshape(-1)
    value_bias_grad = jnp.sum(kv_low_share[:, head_size:].astype(f32), axis=0)
    late = everyone_sum(jnp.concatenate([late, value_bias_grad]), ("tp",))
    late = everyone_sum(jnp.concatenate([late, q_bias_grad]), ("ctx", "fsdp"))
    return (
        layer_out,
        input_grad,
        late[:width],
        late[width : 2 * width],
        q_w_grad,
        late[2 * width + head_size :],
        kv_w_grad,
        late[2 * width : 2 * width + head_size],
        out_w_grad,
        early[1],
        early[2],
        early[3],
        up_w_grad,
        up_bias_out,
        down_w_grad,
        early[0],
    )


def solution(mesh):
    whole = P()
    rows = P(("fsdp", "ctx"), None)
    split = P(("fsdp", "ctx"), "tp")
    turned = P("tp", ("fsdp", "ctx"))
    thin = P(("fsdp", "ctx", "tp"), None)
    in_specs = (
        rows, P("fsdp"), P("fsdp", None), whole, whole, split, P("tp"), rows, whole,
        turned, whole, whole, whole, split, P("tp"), turned, whole, rows,
    )
    out_specs = (
        thin, thin, whole, whole, split, P("tp"), thin, whole, turned, whole, whole, whole,
        split, P("tp"), turned, whole,
    )
    return jax.shard_map(body, mesh=mesh, in_specs=in_specs, out_specs=out_specs, check_vma=False)
```

```python
import math

import jax
import jax.numpy as jnp
import numpy as np
from jax import lax
from jax.experimental import pallas as pl
from jax.experimental.pallas import tpu as pltpu
from jax.sharding import PartitionSpec as P

eps = 1e-05
masked_score = -1000000000.0
f32 = jnp.float32
bf16 = jnp.bfloat16
ring_axes = ("fsdp", "ctx")


def ring_order(rows, cols):
    if rows == 1:
        return list(range(cols))
    if cols == 1:
        return list(range(rows))
    if rows % 2 == 0:
        walk = [(0, c) for c in range(cols)]
        for step, c in enumerate(range(cols - 1, -1, -1)):
            span = range(1, rows) if step % 2 == 0 else range(rows - 1, 0, -1)
            walk += [(r, c) for r in span]
        if cols % 2 == 0 or rows == 2:
            return [r * cols + c for r, c in walk]
    return list(range(rows * cols))


def after(value, gate):
    if gate is None:
        return value
    return lax.optimization_barrier((value, gate))[0]


class Ring:
    def __init__(self, rows, cols, place):
        self.size = rows * cols
        order = ring_order(rows, cols)
        where = [0] * self.size
        for spot, owner in enumerate(order):
            where[owner] = spot
        n = self.size
        self.right = [(order[i], order[(i + 1) % n]) for i in range(n)]
        self.left = [(b, a) for a, b in self.right]
        spot = jnp.asarray(np.array(where, np.int32))[place]
        self.slots = jnp.asarray(np.array(order, np.int32))[
            lax.rem(spot - jnp.arange(n, dtype=jnp.int32) + n, n)
        ]
        self.homes = lax.rem(spot - jnp.asarray(np.array(where, np.int32)) + n, n)

    def hops(self, flip):
        far = self.size // 2
        near = self.size - 1 - far
        return (near, far) if flip else (far, near)

    def gather(self, shard, flip, gate_right=None, gate_left=None):
        hops_right, hops_left = self.hops(flip)
        slots = [shard] * self.size
        moving = after(shard, gate_right)
        for k in range(1, hops_right + 1):
            moving = lax.ppermute(moving, ring_axes, self.right)
            slots[k] = moving
        moving = after(shard, gate_left)
        for k in range(1, hops_left + 1):
            moving = lax.ppermute(moving, ring_axes, self.left)
            slots[self.size - k] = moving
        return slots

    def scatter(self, part, flip):
        hops_right, hops_left = self.hops(flip)
        n = self.size
        total = part(0)
        for hops, sign, pairs in ((hops_right, -1, self.right), (hops_left, 1, self.left)):
            moving = None
            for k in range(hops, 0, -1):
                piece = part((sign * k) % n)
                if moving is not None:
                    piece = piece + moving.astype(f32)
                moving = lax.ppermute(piece.astype(bf16), ring_axes, pairs)
            if moving is not None:
                total = total + moving.astype(f32)
        return total

    def into(self, values):
        width = values.shape[-1] // self.size
        return jnp.concatenate(
            [
                lax.dynamic_slice_in_dim(values, self.slots[k] * width, width, values.ndim - 1)
                for k in range(self.size)
            ],
            axis=-1,
        )

    def back(self, values):
        width = values.shape[-1] // self.size
        return jnp.concatenate(
            [
                lax.dynamic_slice_in_dim(values, self.homes[k] * width, width, values.ndim - 1)
                for k in range(self.size)
            ],
            axis=-1,
        )


def swap(values, axis, bit):
    count = lax.axis_size(axis)
    return lax.ppermute(values, axis, [(i, i ^ bit) for i in range(count)])


def bits_of(axis):
    count = lax.axis_size(axis)
    bit = 1
    while bit < count:
        yield bit
        bit *= 2


def share_sum(keep, send, groups=1):
    width = keep.shape[-1]
    for bit in bits_of("tp"):
        total = keep.astype(f32) + swap(send, "tp", bit).astype(f32)
        if 2 * bit == lax.axis_size("tp"):
            return total
        halves = total.reshape(groups, 2, -1, width)
        keep = halves[:, 0].reshape(-1, width)
        send = halves[:, 1].reshape(-1, width).astype(bf16)


def share_spread(rows):
    for bit in reversed(list(bits_of("tp"))):
        rows = jnp.concatenate([rows, swap(rows, "tp", bit)], axis=0)
    return rows


def everyone_sum(values, axes):
    for axis in axes:
        for bit in bits_of(axis):
            values = values + swap(values, axis, bit)
    return values


def dot(left, right, dims):
    return lax.dot_general(left, right, (dims, ((), ())), preferred_element_type=f32)


NN = ((1,), (0,))
NT = ((1,), (1,))
TN = ((0,), (0,))


def normed(values):
    center = jnp.mean(values, axis=-1, keepdims=True)
    centred = values - center
    spread = jnp.mean(centred * centred, axis=-1, keepdims=True)
    inv = lax.rsqrt(spread + eps)
    return centred * inv, inv


def normed_back(grad, gain, norm, inv):
    pulled = grad * gain
    term = pulled - jnp.mean(pulled, axis=-1, keepdims=True)
    return inv * (term - norm * jnp.mean(pulled * norm, axis=-1, keepdims=True))


def params(megabytes):
    return pltpu.CompilerParams(vmem_limit_bytes=megabytes << 20)


def cost(flops, moved, heavy=0):
    return pl.CostEstimate(flops=flops, bytes_accessed=moved, transcendentals=heavy)


def arrange(values, gain, shift, ring, row_blocks):
    rows, width = values.shape
    blocks = row_blocks.shape[0]
    pieces = ring.size
    share = rows // blocks
    piece = width // pieces
    norm = gain is not None
    moved = piece % 128 == 0
    if not moved:
        values = ring.into(values)
        if norm:
            gain, shift = ring.into(gain), ring.into(shift)

    def source(slot_ref, k):
        if not moved:
            return slice(k * piece, (k + 1) * piece)
        return pl.ds(pl.multiple_of(slot_ref[k] * piece, piece), piece)

    def kernel(slot_ref, block_ref, *refs):
        del block_ref
        if norm:
            in_ref, gain_ref, shift_ref, share_ref, act_ref, natural = refs
        else:
            in_ref, share_ref = refs
        for k in range(pieces):
            from_cols = source(slot_ref, k)
            cols = slice(k * piece, (k + 1) * piece)
            if norm:
                @pl.when(pl.program_id(0) == 0)
                def _(cols=cols, from_cols=from_cols):
                    share_ref[:, cols] = in_ref[:, from_cols]
            else:
                share_ref[:, cols] = in_ref[:, from_cols]
        if norm:
            unit, _ = normed(in_ref[...].astype(f32))
            natural[...] = (unit * gain_ref[...] + shift_ref[...]).astype(bf16)
            for k in range(pieces):
                from_cols = source(slot_ref, k)
                act_ref[:, k * piece : (k + 1) * piece] = natural[:, from_cols]

    row_in = pl.BlockSpec((share, width), lambda i, s, b: (b[i], 0))
    row_out = pl.BlockSpec((share, width), lambda i, s, b: (i, 0))
    first = pl.BlockSpec((share, width), lambda i, s, b: (0, 0))
    line = pl.BlockSpec((1, width), lambda i, s, b: (0, 0))
    full = jax.ShapeDtypeStruct((rows, width), bf16)
    return pl.pallas_call(
        kernel,
        out_shape=(jax.ShapeDtypeStruct((share, width), bf16), full) if norm else full,
        grid_spec=pltpu.PrefetchScalarGridSpec(
            num_scalar_prefetch=2,
            grid=(blocks,),
            in_specs=[row_in, line, line] if norm else [row_in],
            out_specs=(first, row_out) if norm else row_out,
            scratch_shapes=[pltpu.VMEM((share, width), bf16)] if norm else [],
        ),
        compiler_params=params(24),
        cost_estimate=cost(10 * rows * width, 4 * rows * width),
    )(ring.slots, row_blocks, values, *((gain, shift) if norm else ()))


def slot_list(chunks, axis):
    if chunks[0].shape[axis] % 128 != 0:
        return [jnp.concatenate(chunks, axis=axis)]
    return chunks


def chunk_sum(left, chunks, turned, tile, extras, finish, outs, megabytes=40):
    chunks = slot_list(chunks, 1 if turned else 0)
    rows, depth = left.shape
    count = len(chunks)
    piece = depth // count
    columns = chunks[0].shape[0 if turned else 1]
    tile = min(tile, columns)

    def kernel(*refs):
        left_ref = refs[0]
        chunk_refs = refs[1 : 1 + count]
        extra_refs = refs[1 + count : 1 + count + len(extras)]
        out_refs = refs[1 + count + len(extras) :]
        total = None
        for k in range(count):
            part = dot(left_ref[:, k * piece : (k + 1) * piece], chunk_refs[k][...], NT if turned else NN)
            total = part if total is None else total + part
        finish(total, extra_refs, out_refs)

    if turned:
        chunk_spec = pl.BlockSpec((tile, piece), lambda i: (i, 0))
    else:
        chunk_spec = pl.BlockSpec((piece, tile), lambda i: (0, i))
    return pl.pallas_call(
        kernel,
        out_shape=tuple(jax.ShapeDtypeStruct((r, columns), d) for d, r in outs),
        grid=(columns // tile,),
        in_specs=[pl.BlockSpec((rows, depth), lambda i: (0, 0))]
        + [chunk_spec] * count
        + [pl.BlockSpec((r, tile), lambda i: (0, i)) for _, r in extras],
        out_specs=tuple(pl.BlockSpec((r, tile), lambda i: (0, i)) for _, r in outs),
        compiler_params=params(megabytes),
        cost_estimate=cost(
            2 * rows * depth * columns, 2 * (rows * depth + depth * columns) + 8 * rows * columns
        ),
    )(left, *chunks, *(a for a, _ in extras))


def chunk_side(left, chunks, turned, megabytes=40):
    chunks = slot_list(chunks, 0 if turned else 1)
    rows, depth = left.shape
    count = len(chunks)
    piece = chunks[0].shape[0 if turned else 1]
    block = (piece, depth) if turned else (depth, piece)
    half = rows // 2

    def kernel(*refs):
        left_ref = refs[0]
        chunk_refs = refs[1 : 1 + count]
        keep_ref, send_ref, held, sems = refs[1 + count :]
        def copy(k):
            source = chunk_refs[k]
            if chunk_refs[k].shape != block:
                source = source.at[:, :depth] if turned else source.at[:depth, :]
            return pltpu.make_async_copy(source, held.at[k], sems.at[k])
        for k in range(count):
            copy(k).start()
        for k in range(count):
            copy(k).wait()
            part = dot(left_ref[...], held[k], NT if turned else NN).astype(bf16)
            keep_ref[:, k * piece : (k + 1) * piece] = part[:half]
            send_ref[:, k * piece : (k + 1) * piece] = part[half:]

    shape = jax.ShapeDtypeStruct((half, piece * count), bf16)
    return pl.pallas_call(
        kernel,
        out_shape=(shape, shape),
        in_specs=[pl.BlockSpec(memory_space=pltpu.VMEM)]
        + [pl.BlockSpec(memory_space=pl.ANY)] * count,
        out_specs=(pl.BlockSpec(memory_space=pltpu.VMEM),) * 2,
        scratch_shapes=[pltpu.VMEM((count,) + block, bf16), pltpu.SemaphoreType.DMA((count,))],
        compiler_params=params(megabytes),
        cost_estimate=cost(
            2 * rows * depth * piece * count,
            2 * (rows * depth + depth * piece * count + rows * piece * count),
        ),
    )(left, *chunks)


def mask_of(info_ref, key_ref, keys):
    own, one, two, place = (info_ref[i : i + 1, :] for i in range(4))
    seg = key_ref[keys, 0:1]
    spot = key_ref[keys, 1:2]
    return ((seg == own) | (seg == one) | (seg == two)) & (spot <= place)


def attend(qkv, kv_blocks, key_info, query_info, heads, head, scale, rows_at_once=256):
    rows = qkv.shape[0]
    count = len(kv_blocks)
    span = kv_blocks[0].shape[0]
    keys = span * count

    def kernel(q_ref, *refs):
        kv_refs = refs[:count]
        key_ref, info_ref, out_ref, log_ref, turned, score, exps = refs[count:]

        @pl.when(pl.program_id(0) == 0)
        def _():
            for d in range(count):
                turned[:, d * span : (d + 1) * span] = kv_refs[d][:, head:].T

        masks = [
            mask_of(info_ref, key_ref, slice(d * span, (d + 1) * span)) for d in range(count)
        ]
        for h in range(heads):
            query = q_ref[:, h * head : (h + 1) * head]
            top = None
            for d in range(count):
                raw = dot(kv_refs[d][:, :head], query, NT) * scale
                raw = jnp.where(masks[d], raw, masked_score)
                score[d * span : (d + 1) * span, :] = raw
                peak = jnp.max(raw, axis=0, keepdims=True)
                top = peak if top is None else jnp.maximum(top, peak)
            total = None
            for d in range(count):
                e = jnp.exp(score[d * span : (d + 1) * span, :] - top)
                exps[d * span : (d + 1) * span, :] = e
                summed = jnp.sum(e, axis=0, keepdims=True)
                total = summed if total is None else total + summed
            mixed = None
            inverse = 1.0 / total
            for d in range(count):
                low = (exps[d * span : (d + 1) * span, :] * inverse).astype(bf16)
                part = dot(turned[:, d * span : (d + 1) * span], low, NN)
                mixed = part if mixed is None else mixed + part
            out_ref[:, h * head : (h + 1) * head] = mixed.T.astype(bf16)
            log_ref[h : h + 1, :] = top + jnp.log(total)

    block = rows_at_once
    return pl.pallas_call(
        kernel,
        out_shape=(
            jax.ShapeDtypeStruct((rows, heads * head), bf16),
            jax.ShapeDtypeStruct((8, rows), f32),
        ),
        grid=(rows // block,),
        in_specs=[pl.BlockSpec((block, heads * head), lambda i: (i, 0))]
        + [pl.BlockSpec((span, 2 * head), lambda i: (0, 0))] * count
        + [
            pl.BlockSpec((keys, 2), lambda i: (0, 0)),
            pl.BlockSpec((8, block), lambda i: (0, i)),
        ],
        out_specs=(
            pl.BlockSpec((block, heads * head), lambda i: (i, 0)),
            pl.BlockSpec((8, block), lambda i: (0, i)),
        ),
        scratch_shapes=[
            pltpu.VMEM((head, keys), bf16),
            pltpu.VMEM((keys, block), f32),
            pltpu.VMEM((keys, block), f32),
        ],
        compiler_params=params(40),
        cost_estimate=cost(4 * rows * keys * heads * head, 4 * rows * heads * head, rows * keys * heads),
    )(qkv, *kv_blocks, key_info, query_info)


def attend_back(qkv, kv_blocks, key_info, query_info, logs, grad, heads, head, scale, rows_at_once=256):
    rows = qkv.shape[0]
    count = len(kv_blocks)
    span = kv_blocks[0].shape[0]
    keys = span * count

    def kernel(q_ref, *refs):
        kv_refs = refs[:count]
        key_ref, info_ref, log_ref, grad_ref, dq_ref, dkv_ref, turned, probs, pulls = refs[count:]

        @pl.when(pl.program_id(0) == 0)
        def _():
            for d in range(count):
                turned[:, d * span : (d + 1) * span] = kv_refs[d][:, :head].T
            dkv_ref[...] = jnp.zeros_like(dkv_ref)

        masks = [
            mask_of(info_ref, key_ref, slice(d * span, (d + 1) * span)) for d in range(count)
        ]
        for h in range(heads):
            cols = slice(h * head, (h + 1) * head)
            query = q_ref[:, cols]
            pulled = grad_ref[:, cols]
            log = log_ref[h : h + 1, :]
            delta = None
            for d in range(count):
                at = slice(d * span, (d + 1) * span)
                raw = dot(kv_refs[d][:, :head], query, NT) * scale
                p = jnp.exp(jnp.where(masks[d], raw, masked_score) - log)
                g = dot(kv_refs[d][:, head:], pulled, NT)
                probs[at, :] = p
                pulls[at, :] = g
                part = jnp.sum(p * g, axis=0, keepdims=True)
                delta = part if delta is None else delta + part
                dkv_ref[at, head:] += dot(p.astype(bf16), pulled, NN)
            mixed = None
            for d in range(count):
                at = slice(d * span, (d + 1) * span)
                ds = (probs[at, :] * (pulls[at, :] - delta)).astype(bf16)
                dkv_ref[at, :head] += dot(ds, query, NN) * scale
                part = dot(turned[:, at], ds, NN)
                mixed = part if mixed is None else mixed + part
            dq_ref[:, cols] = (mixed * scale).T.astype(bf16)

    block = rows_at_once
    return pl.pallas_call(
        kernel,
        out_shape=(
            jax.ShapeDtypeStruct((rows, heads * head), bf16),
            jax.ShapeDtypeStruct((keys, 2 * head), f32),
        ),
        grid=(rows // block,),
        in_specs=[pl.BlockSpec((block, heads * head), lambda i: (i, 0))]
        + [pl.BlockSpec((span, 2 * head), lambda i: (0, 0))] * count
        + [
            pl.BlockSpec((keys, 2), lambda i: (0, 0)),
            pl.BlockSpec((8, block), lambda i: (0, i)),
            pl.BlockSpec((8, block), lambda i: (0, i)),
            pl.BlockSpec((block, heads * head), lambda i: (i, 0)),
        ],
        out_specs=(
            pl.BlockSpec((block, heads * head), lambda i: (i, 0)),
            pl.BlockSpec((keys, 2 * head), lambda i: (0, 0)),
        ),
        scratch_shapes=[
            pltpu.VMEM((head, keys), bf16),
            pltpu.VMEM((keys, block), f32),
            pltpu.VMEM((keys, block), f32),
        ],
        compiler_params=params(44),
        cost_estimate=cost(
            10 * rows * keys * heads * head, 8 * keys * head + 6 * rows * heads * head, rows * keys * heads
        ),
    )(qkv, *kv_blocks, key_info, query_info, logs, grad)


def parent_lookup(seg_ids, parents):
    labels = jnp.arange(parents.shape[0], dtype=jnp.int32)
    picked = jnp.where(seg_ids[:, None] == labels[None, :], parents[None, :], 0)
    return jnp.sum(picked, axis=1)


def gelu_parts(values):
    scale = math.sqrt(2.0 / math.pi)
    squared = values * values
    bend = jnp.tanh(scale * (values + 0.044715 * squared * values))
    out = 0.5 * values * (1.0 + bend)
    slope = 0.5 * (1.0 + bend) + 0.5 * values * (1.0 - bend * bend) * scale * (
        1.0 + 3 * 0.044715 * squared
    )
    return out, slope


def body(
    tokens,
    token_segment,
    segment_parent,
    ln1_gain,
    ln1_bias,
    q_weight,
    q_bias,
    kv_weight,
    value_bias,
    o_weight,
    o_bias,
    ln2_gain,
    ln2_bias,
    up_weight,
    up_bias,
    down_weight,
    down_bias,
    out_grad,
):
    row_count, width = tokens.shape
    head_size = value_bias.shape[0]
    local_width = q_weight.shape[1]
    local_heads = local_width // head_size
    tree_length = token_segment.shape[0]
    score_scale = 1.0 / math.sqrt(head_size)
    ctx_count = lax.axis_size("ctx")
    tp_count = lax.axis_size("tp")
    ctx_index = lax.axis_index("ctx")
    tp_index = lax.axis_index("tp")
    share_rows = row_count // tp_count
    ring = Ring(lax.axis_size("fsdp"), ctx_count, lax.axis_index("fsdp") * ctx_count + ctx_index)
    n = ring.size
    piece = width // n

    qkv_slots = ring.gather(jnp.concatenate([q_weight, kv_weight], axis=1), False)
    o_slots = ring.gather(o_weight, True)
    half = n // 2
    up_slots = ring.gather(up_weight, False, o_slots[half - 1], o_slots[half])
    down_slots = ring.gather(down_weight, True, up_slots[2 % n], up_slots[(n - 2) % n])

    masks = [0]
    for bit in reversed(list(bits_of("tp"))):
        masks = masks + [m ^ bit for m in masks]
    row_blocks = [tp_index ^ m for m in masks]

    def rows_in(values):
        return jnp.concatenate(
            [
                lax.dynamic_slice_in_dim(values, b * share_rows, share_rows, 0)
                for b in row_blocks
            ],
            axis=0,
        )

    row_ids = jnp.stack(row_blocks)
    x_low_share, act_one = arrange(
        tokens, ln1_gain.astype(f32)[None], ln1_bias.astype(f32)[None], ring, row_ids
    )
    g_low = arrange(out_grad, None, None, ring, row_ids)
    vectors = ring.into(
        jnp.stack([ln1_gain, ln1_bias, o_bias, ln2_gain, ln2_bias, down_bias]).astype(f32)
    )
    gain_one, _, o_shift, gain_two, shift_two, down_shift = (
        vectors[i : i + 1] for i in range(6)
    )
    own_place = rows_in(jnp.arange(row_count, dtype=jnp.int32))

    parents = segment_parent[0]
    query_place = ctx_index * row_count + own_place
    key_places = []
    for d in range(ctx_count):
        start = (ctx_index - d) * row_count
        key_places.append(jnp.where(start >= 0, start + own_place, tree_length))
    key_place = jnp.concatenate(key_places)
    segment_blocks = rows_in(token_segment.reshape(ctx_count, row_count).T)
    own_seg = lax.dynamic_slice_in_dim(segment_blocks, ctx_index, 1, 1)[:, 0]
    key_segment = jnp.concatenate(
        [
            lax.dynamic_slice_in_dim(
                segment_blocks, lax.rem(ctx_index - d + ctx_count, ctx_count), 1, 1
            )[:, 0]
            for d in range(ctx_count)
        ]
    )
    seg_one = parent_lookup(own_seg, parents)
    seg_two = parent_lookup(seg_one, parents)
    key_info = jnp.stack([key_segment, key_place], axis=1)
    blank = jnp.zeros_like(own_seg)
    query_info = jnp.stack([own_seg, seg_one, seg_two, query_place, blank, blank, blank, blank])

    qkv_shift = jnp.concatenate(
        [q_bias.astype(f32), jnp.zeros((head_size,), f32), value_bias.astype(f32)]
    )

    def add_shift(total, extra, out):
        out[0][...] = (total + extra[0][...]).astype(bf16)

    (qkv,) = chunk_sum(
        act_one, qkv_slots, False, 256, [(qkv_shift[None], 1)], add_shift, [(bf16, row_count)]
    )
    kv_own = qkv[:, local_width:]
    kv_blocks = [kv_own] + [
        lax.ppermute(kv_own, "ctx", [(c, c + d) for c in range(ctx_count - d)])
        for d in range(1, ctx_count)
    ]
    attended, logs = attend(
        qkv, kv_blocks, key_info, query_info, local_heads, head_size, score_scale
    )
    attn_share = share_sum(*chunk_side(attended, o_slots, False))
    x_share = x_low_share.astype(f32)
    residual = x_share + (attn_share + o_shift)
    norm_two, inv_two = normed(residual)
    act_two = share_spread((norm_two * gain_two + shift_two).astype(bf16))


    def activate(total, extra, out):
        gelu_out, gelu_slope = gelu_parts(total + extra[0][...])
        out[0][...] = gelu_out.astype(bf16)
        out[1][...] = gelu_slope

    hidden, gelu_slope = chunk_sum(
        act_two,
        up_slots,
        False,
        256,
        [(up_bias.astype(f32)[None], 1)],
        activate,
        [(bf16, row_count), (f32, row_count)],
    )
    down_w_grad = ring.scatter(
        lambda k: dot(hidden, g_low[:, k * piece : (k + 1) * piece], TN), False
    )

    def deactivate(total, extra, out):
        low = (total * extra[0][...]).astype(bf16)
        out[0][...] = low
        out[1][...] = jnp.sum(low.astype(f32), axis=0, keepdims=True)

    grad_pre, up_bias_grad = chunk_sum(
        g_low,
        down_slots,
        True,
        256,
        [(gelu_slope, row_count)],
        deactivate,
        [(bf16, row_count), (f32, 1)],
    )
    up_bias_grad = up_bias_grad[0]
    up_w_grad = ring.scatter(
        lambda k: dot(act_two[:, k * piece : (k + 1) * piece], grad_pre, TN), True
    )
    grad_two = share_sum(*chunk_side(grad_pre, up_slots, True))
    ffn_share = share_sum(*chunk_side(hidden, down_slots, False))
    layer_out = ring.back((residual + (ffn_share + down_shift)).astype(bf16))

    g_share = g_low[:share_rows].astype(f32)
    grad_res = g_share + normed_back(grad_two, gain_two, norm_two, inv_two)
    grad_attn_share = grad_res.astype(bf16)
    grad_attn = share_spread(grad_attn_share)
    out_w_grad = ring.scatter(
        lambda k: dot(attended, grad_attn[:, k * piece : (k + 1) * piece], TN), False
    )

    def only_round(total, extra, out):
        out[0][...] = total.astype(bf16)

    (grad_attended,) = chunk_sum(
        grad_attn, o_slots, True, 256, [], only_round, [(bf16, row_count)]
    )
    early = jnp.stack(
        [
            jnp.sum(g_share, axis=0),
            jnp.sum(grad_attn_share.astype(f32), axis=0),
            jnp.sum(grad_two * norm_two, axis=0),
            jnp.sum(grad_two, axis=0),
        ]
    )
    early = everyone_sum(ring.back(early).reshape(-1), ("tp",))

    grad_query, kv_grad = attend_back(
        qkv, kv_blocks, key_info, query_info, logs, grad_attended,
        local_heads, head_size, score_scale,
    )
    q_bias_grad = jnp.sum(grad_query.astype(f32), axis=0)

    kv_part = kv_grad.astype(bf16).reshape(ctx_count, 2, row_count // 2, 2 * head_size)
    kv_part = share_sum(
        kv_part[:, 0].reshape(-1, 2 * head_size),
        kv_part[:, 1].reshape(-1, 2 * head_size),
        ctx_count,
    ).reshape(ctx_count, share_rows, 2 * head_size)
    kv_sum = kv_part[0]
    for d in range(1, ctx_count):
        kv_sum = kv_sum + lax.ppermute(
            kv_part[d].astype(bf16), "ctx", [(c, c - d) for c in range(d, ctx_count)]
        ).astype(f32)
    kv_low_share = kv_sum.astype(bf16)
    kv_low = share_spread(kv_low_share)

    sub = piece // tp_count

    def q_kv_part(k):
        act_piece = act_one[:, k * piece : (k + 1) * piece]
        q_piece = dot(act_piece, grad_query, TN)
        kv_piece = lax.dynamic_slice_in_dim(dot(act_piece, kv_low, TN), tp_index * sub, sub, 0)
        kv_piece = jnp.concatenate([kv_piece[: sub // 2], kv_piece[sub // 2 :]], axis=1)
        return jnp.concatenate([q_piece, kv_piece], axis=0)

    q_kv = ring.scatter(q_kv_part, True)
    q_w_grad = q_kv[:piece]
    kv_w_grad = jnp.concatenate(
        [q_kv[piece:, : 2 * head_size], q_kv[piece:, 2 * head_size :]], axis=0
    )

    kv_full = jnp.concatenate([c[:, local_width:] for c in qkv_slots], axis=0)
    grad_act = share_sum(*chunk_side(grad_query, qkv_slots, True)) + dot(
        kv_low_share, kv_full, NT
    )
    norm_share, inv_share = normed(x_share)
    input_grad = ring.back(
        (grad_res + normed_back(grad_act, gain_one, norm_share, inv_share)).astype(bf16)
    )
    late = jnp.stack([jnp.sum(grad_act * norm_share, axis=0), jnp.sum(grad_act, axis=0)])
    late = ring.back(late).reshape(-1)
    value_bias_grad = jnp.sum(kv_low_share[:, head_size:].astype(f32), axis=0)
    late = everyone_sum(jnp.concatenate([late, value_bias_grad]), ("tp",))
    sums = [late, early, q_bias_grad, up_bias_grad]
    cuts = np.cumsum([v.shape[0] for v in sums])
    sums = everyone_sum(jnp.concatenate(sums), ("ctx", "fsdp"))
    late, early, q_bias_out, up_bias_out = (
        sums[stop - v.shape[0] : stop]
        for stop, v in zip(cuts, (late, early, q_bias_grad, up_bias_grad))
    )
    early = early.reshape(4, width)
    return (
        layer_out,
        input_grad,
        late[:width],
        late[width : 2 * width],
        q_w_grad,
        q_bias_out,
        kv_w_grad,
        late[2 * width :],
        out_w_grad,
        early[1],
        early[2],
        early[3],
        up_w_grad,
        up_bias_out,
        down_w_grad,
        early[0],
    )


def solution(mesh):
    whole = P()
    rows = P(("fsdp", "ctx"), None)
    split = P(("fsdp", "ctx"), "tp")
    turned = P("tp", ("fsdp", "ctx"))
    thin = P(("fsdp", "ctx", "tp"), None)
    in_specs = (
        rows, P("fsdp"), P("fsdp", None), whole, whole, split, P("tp"), rows, whole,
        turned, whole, whole, whole, split, P("tp"), turned, whole, rows,
    )
    out_specs = (
        thin, thin, whole, whole, split, P("tp"), thin, whole, turned, whole, whole, whole,
        split, P("tp"), turned, whole,
    )
    return jax.shard_map(body, mesh=mesh, in_specs=in_specs, out_specs=out_specs, check_vma=False)
```

```python
import math

import jax
import jax.numpy as jnp
import numpy as np
from jax import lax
from jax.experimental import pallas as pl
from jax.experimental.pallas import tpu as pltpu
from jax.sharding import PartitionSpec as P

eps = 1e-05
masked_score = -1000000000.0
log2_e = math.log2(math.e)
f32 = jnp.float32
bf16 = jnp.bfloat16
ring_axes = ("fsdp", "ctx")


def ring_order(rows, cols):
    if rows == 1:
        return list(range(cols))
    if cols == 1:
        return list(range(rows))
    if rows % 2 == 0:
        walk = [(0, c) for c in range(cols)]
        for step, c in enumerate(range(cols - 1, -1, -1)):
            span = range(1, rows) if step % 2 == 0 else range(rows - 1, 0, -1)
            walk += [(r, c) for r in span]
        if cols % 2 == 0 or rows == 2:
            return [r * cols + c for r, c in walk]
    return list(range(rows * cols))


def after(value, gate):
    if gate is None:
        return value
    return lax.optimization_barrier((value, gate))[0]


class Ring:
    def __init__(self, rows, cols, place):
        self.size = rows * cols
        order = ring_order(rows, cols)
        where = [0] * self.size
        for spot, owner in enumerate(order):
            where[owner] = spot
        n = self.size
        self.right = [(order[i], order[(i + 1) % n]) for i in range(n)]
        self.left = [(b, a) for a, b in self.right]
        spot = jnp.asarray(np.array(where, np.int32))[place]
        self.slots = jnp.asarray(np.array(order, np.int32))[
            lax.rem(spot - jnp.arange(n, dtype=jnp.int32) + n, n)
        ]
        self.homes = lax.rem(spot - jnp.asarray(np.array(where, np.int32)) + n, n)

    def hops(self, flip):
        far = self.size // 2
        near = self.size - 1 - far
        return (near, far) if flip else (far, near)

    def gather(self, shard, flip, gate_right=None, gate_left=None):
        hops_right, hops_left = self.hops(flip)
        slots = [shard] * self.size
        moving = after(shard, gate_right)
        for k in range(1, hops_right + 1):
            moving = lax.ppermute(moving, ring_axes, self.right)
            slots[k] = moving
        moving = after(shard, gate_left)
        for k in range(1, hops_left + 1):
            moving = lax.ppermute(moving, ring_axes, self.left)
            slots[self.size - k] = moving
        return slots

    def scatter(self, part, flip):
        hops_right, hops_left = self.hops(flip)
        n = self.size
        last = []
        for hops, sign, pairs in ((hops_right, -1, self.right), (hops_left, 1, self.left)):
            moving = None
            for k in range(hops, 0, -1):
                piece = part((sign * k) % n)
                if moving is not None:
                    piece = piece + moving.astype(f32)
                moving = lax.ppermute(piece.astype(bf16), ring_axes, pairs)
            if moving is not None:
                last.append(moving)

        def finish(gate=None):
            total = part(0)
            for moving in last:
                total = total + after(moving, gate).astype(f32)
            return total

        return finish

    def into(self, values):
        width = values.shape[-1] // self.size
        return jnp.concatenate(
            [
                lax.dynamic_slice_in_dim(values, self.slots[k] * width, width, values.ndim - 1)
                for k in range(self.size)
            ],
            axis=-1,
        )

    def back(self, values):
        width = values.shape[-1] // self.size
        return jnp.concatenate(
            [
                lax.dynamic_slice_in_dim(values, self.homes[k] * width, width, values.ndim - 1)
                for k in range(self.size)
            ],
            axis=-1,
        )


def swap(values, axis, bit):
    count = lax.axis_size(axis)
    return lax.ppermute(values, axis, [(i, i ^ bit) for i in range(count)])


def bits_of(axis):
    count = lax.axis_size(axis)
    bit = 1
    while bit < count:
        yield bit
        bit *= 2


def share_sum(keep, send, groups=1):
    width = keep.shape[-1]
    for bit in bits_of("tp"):
        total = keep.astype(f32) + swap(send, "tp", bit).astype(f32)
        if 2 * bit == lax.axis_size("tp"):
            return total
        halves = total.reshape(groups, 2, -1, width)
        keep = halves[:, 0].reshape(-1, width)
        send = halves[:, 1].reshape(-1, width).astype(bf16)


def share_spread(rows):
    for bit in reversed(list(bits_of("tp"))):
        rows = jnp.concatenate([rows, swap(rows, "tp", bit)], axis=0)
    return rows


def everyone_sum(values, axes):
    for axis in axes:
        for bit in bits_of(axis):
            values = values + swap(values, axis, bit)
    return values


def dot(left, right, dims):
    return lax.dot_general(left, right, (dims, ((), ())), preferred_element_type=f32)


NN = ((1,), (0,))
NT = ((1,), (1,))
TN = ((0,), (0,))


def normed(values):
    center = jnp.mean(values, axis=-1, keepdims=True)
    centred = values - center
    spread = jnp.mean(centred * centred, axis=-1, keepdims=True)
    inv = lax.rsqrt(spread + eps)
    return centred * inv, inv


def normed_back(grad, gain, norm, inv):
    pulled = grad * gain
    term = pulled - jnp.mean(pulled, axis=-1, keepdims=True)
    return inv * (term - norm * jnp.mean(pulled * norm, axis=-1, keepdims=True))


def params(megabytes):
    return pltpu.CompilerParams(vmem_limit_bytes=megabytes << 20)


def cost(flops, moved, heavy=0):
    return pl.CostEstimate(flops=flops, bytes_accessed=moved, transcendentals=heavy)


def arrange(values, gain, shift, ring, row_blocks):
    rows, width = values.shape
    blocks = row_blocks.shape[0]
    pieces = ring.size
    share = rows // blocks
    piece = width // pieces
    norm = gain is not None
    moved = piece % 128 == 0
    if not moved:
        values = ring.into(values)
        if norm:
            gain, shift = ring.into(gain), ring.into(shift)

    def source(slot_ref, k):
        if not moved:
            return slice(k * piece, (k + 1) * piece)
        return pl.ds(pl.multiple_of(slot_ref[k] * piece, piece), piece)

    def kernel(slot_ref, block_ref, *refs):
        del block_ref
        if norm:
            in_ref, gain_ref, shift_ref, share_ref, act_ref, natural = refs
        else:
            in_ref, share_ref = refs
        for k in range(pieces):
            from_cols = source(slot_ref, k)
            cols = slice(k * piece, (k + 1) * piece)
            if norm:
                @pl.when(pl.program_id(0) == 0)
                def _(cols=cols, from_cols=from_cols):
                    share_ref[:, cols] = in_ref[:, from_cols]
            else:
                share_ref[:, cols] = in_ref[:, from_cols]
        if norm:
            unit, _ = normed(in_ref[...].astype(f32))
            natural[...] = (unit * gain_ref[...] + shift_ref[...]).astype(bf16)
            for k in range(pieces):
                from_cols = source(slot_ref, k)
                act_ref[:, k * piece : (k + 1) * piece] = natural[:, from_cols]

    row_in = pl.BlockSpec((share, width), lambda i, s, b: (b[i], 0))
    row_out = pl.BlockSpec((share, width), lambda i, s, b: (i, 0))
    first = pl.BlockSpec((share, width), lambda i, s, b: (0, 0))
    line = pl.BlockSpec((1, width), lambda i, s, b: (0, 0))
    full = jax.ShapeDtypeStruct((rows, width), bf16)
    return pl.pallas_call(
        kernel,
        out_shape=(jax.ShapeDtypeStruct((share, width), bf16), full) if norm else full,
        grid_spec=pltpu.PrefetchScalarGridSpec(
            num_scalar_prefetch=2,
            grid=(blocks,),
            in_specs=[row_in, line, line] if norm else [row_in],
            out_specs=(first, row_out) if norm else row_out,
            scratch_shapes=[pltpu.VMEM((share, width), bf16)] if norm else [],
        ),
        compiler_params=params(24),
        cost_estimate=cost(10 * rows * width, 4 * rows * width),
    )(ring.slots, row_blocks, values, *((gain, shift) if norm else ()))


def slot_list(chunks, axis):
    if chunks[0].shape[axis] % 128 != 0:
        return [jnp.concatenate(chunks, axis=axis)]
    return chunks


def chunk_sum(left, chunks, turned, tile, extras, finish, outs, megabytes=40):
    chunks = slot_list(chunks, 1 if turned else 0)
    rows, depth = left.shape
    count = len(chunks)
    piece = depth // count
    columns = chunks[0].shape[0 if turned else 1]
    tile = min(tile, columns)

    def kernel(*refs):
        left_ref = refs[0]
        chunk_refs = refs[1 : 1 + count]
        extra_refs = refs[1 + count : 1 + count + len(extras)]
        out_refs = refs[1 + count + len(extras) :]
        step = min(rows, 256)
        for start in range(0, rows, step):
            at = slice(start, start + step)
            total = None
            for k in range(count):
                part = dot(
                    left_ref[at, k * piece : (k + 1) * piece],
                    chunk_refs[k][...],
                    NT if turned else NN,
                )
                total = part if total is None else total + part
            finish(total, extra_refs, out_refs, at)

    if turned:
        chunk_spec = pl.BlockSpec((tile, piece), lambda i: (i, 0))
    else:
        chunk_spec = pl.BlockSpec((piece, tile), lambda i: (0, i))
    return pl.pallas_call(
        kernel,
        out_shape=tuple(jax.ShapeDtypeStruct((r, columns), d) for d, r in outs),
        grid=(columns // tile,),
        in_specs=[pl.BlockSpec((rows, depth), lambda i: (0, 0))]
        + [chunk_spec] * count
        + [pl.BlockSpec((r, tile), lambda i: (0, i)) for _, r in extras],
        out_specs=tuple(pl.BlockSpec((r, tile), lambda i: (0, i)) for _, r in outs),
        compiler_params=params(megabytes),
        cost_estimate=cost(
            2 * rows * depth * columns, 2 * (rows * depth + depth * columns) + 8 * rows * columns
        ),
    )(left, *chunks, *(a for a, _ in extras))


def chunk_side(left, chunks, turned, megabytes=40):
    chunks = slot_list(chunks, 0 if turned else 1)
    rows, depth = left.shape
    count = len(chunks)
    piece = chunks[0].shape[0 if turned else 1]
    block = (piece, depth) if turned else (depth, piece)
    half = rows // 2

    def kernel(*refs):
        left_ref = refs[0]
        chunk_refs = refs[1 : 1 + count]
        keep_ref, send_ref, held, sems = refs[1 + count :]
        def copy(k):
            source = chunk_refs[k]
            if chunk_refs[k].shape != block:
                source = source.at[:, :depth] if turned else source.at[:depth, :]
            return pltpu.make_async_copy(source, held.at[k], sems.at[k])
        for k in range(count):
            copy(k).start()
        for k in range(count):
            copy(k).wait()
            for out_ref, start in ((keep_ref, 0), (send_ref, half)):
                part = dot(left_ref[start : start + half, :], held[k], NT if turned else NN)
                out_ref[:, k * piece : (k + 1) * piece] = part.astype(bf16)

    shape = jax.ShapeDtypeStruct((half, piece * count), bf16)
    return pl.pallas_call(
        kernel,
        out_shape=(shape, shape),
        in_specs=[pl.BlockSpec(memory_space=pltpu.VMEM)]
        + [pl.BlockSpec(memory_space=pl.ANY)] * count,
        out_specs=(pl.BlockSpec(memory_space=pltpu.VMEM),) * 2,
        scratch_shapes=[pltpu.VMEM((count,) + block, bf16), pltpu.SemaphoreType.DMA((count,))],
        compiler_params=params(megabytes),
        cost_estimate=cost(
            2 * rows * depth * piece * count,
            2 * (rows * depth + depth * piece * count + rows * piece * count),
        ),
    )(left, *chunks)


def mask_of(info_ref, key_ref, keys):
    own, one, two, place = (info_ref[i : i + 1, :] for i in range(4))
    seg = key_ref[keys, 0:1]
    spot = key_ref[keys, 1:2]
    return ((seg == own) | (seg == one) | (seg == two)) & (spot <= place)


def attend(qkv, kv_blocks, key_info, query_info, heads, head, scale, rows_at_once=512):
    rows = qkv.shape[0]
    count = len(kv_blocks)
    span = kv_blocks[0].shape[0]
    keys = span * count

    def kernel(q_ref, *refs):
        kv_refs = refs[:count]
        key_ref, info_ref, out_ref, log_ref, turned, score = refs[count:]

        @pl.when(pl.program_id(0) == 0)
        def _():
            for d in range(count):
                turned[:, d * span : (d + 1) * span] = kv_refs[d][:, head:].T

        masks = [
            mask_of(info_ref, key_ref, slice(d * span, (d + 1) * span)) for d in range(count)
        ]
        for h in range(heads):
            query = q_ref[:, h * head : (h + 1) * head]
            top = None
            for d in range(count):
                raw = dot(kv_refs[d][:, :head], query, NT)
                raw = jnp.where(masks[d], raw, masked_score / scale)
                score[d * span : (d + 1) * span, :] = raw
                peak = jnp.max(raw, axis=0, keepdims=True)
                top = peak if top is None else jnp.maximum(top, peak)
            total = mixed = None
            for d in range(count):
                e = jnp.exp2((score[d * span : (d + 1) * span, :] - top) * (scale * log2_e))
                summed = jnp.sum(e, axis=0, keepdims=True)
                total = summed if total is None else total + summed
                part = dot(turned[:, d * span : (d + 1) * span], e.astype(bf16), NN)
                mixed = part if mixed is None else mixed + part
            out_ref[:, h * head : (h + 1) * head] = (mixed * (1.0 / total)).T.astype(bf16)
            log_ref[h : h + 1, :] = (top * scale + jnp.log(total)) * log2_e

    block = min(rows_at_once, rows)
    return pl.pallas_call(
        kernel,
        out_shape=(
            jax.ShapeDtypeStruct((rows, heads * head), bf16),
            jax.ShapeDtypeStruct((8, rows), f32),
        ),
        grid=(rows // block,),
        in_specs=[pl.BlockSpec((block, heads * head), lambda i: (i, 0))]
        + [pl.BlockSpec((span, 2 * head), lambda i: (0, 0))] * count
        + [
            pl.BlockSpec((keys, 2), lambda i: (0, 0)),
            pl.BlockSpec((8, block), lambda i: (0, i)),
        ],
        out_specs=(
            pl.BlockSpec((block, heads * head), lambda i: (i, 0)),
            pl.BlockSpec((8, block), lambda i: (0, i)),
        ),
        scratch_shapes=[
            pltpu.VMEM((head, keys), bf16),
            pltpu.VMEM((keys, block), f32),
        ],
        compiler_params=params(40),
        cost_estimate=cost(4 * rows * keys * heads * head, 4 * rows * heads * head, rows * keys * heads),
    )(qkv, *kv_blocks, key_info, query_info)


def attend_back(qkv, kv_blocks, key_info, query_info, logs, grad, out, heads, head, scale, rows_at_once=256):
    rows = qkv.shape[0]
    count = len(kv_blocks)
    span = kv_blocks[0].shape[0]
    keys = span * count

    def kernel(q_ref, *refs):
        kv_refs = refs[:count]
        key_ref, info_ref, log_ref, grad_ref, out_ref, dq_ref, dkv_ref, turned = refs[count:]

        @pl.when(pl.program_id(0) == 0)
        def _():
            for d in range(count):
                turned[:, d * span : (d + 1) * span] = kv_refs[d][:, :head].T
            dkv_ref[...] = jnp.zeros_like(dkv_ref)

        masks = [
            mask_of(info_ref, key_ref, slice(d * span, (d + 1) * span)) for d in range(count)
        ]
        for h in range(heads):
            cols = slice(h * head, (h + 1) * head)
            query = q_ref[:, cols]
            pulled = grad_ref[:, cols]
            log = log_ref[h : h + 1, :]
            delta = jnp.sum(
                (pulled.astype(f32) * out_ref[:, cols].astype(f32)).T, axis=0, keepdims=True
            )
            mixed = None
            for d in range(count):
                at = slice(d * span, (d + 1) * span)
                raw = dot(kv_refs[d][:, :head], query, NT) * (scale * log2_e)
                p = jnp.exp2(jnp.where(masks[d], raw, masked_score) - log)
                g = dot(kv_refs[d][:, head:], pulled, NT)
                ds = (p * (g - delta)).astype(bf16)
                dkv_ref[at, head:] += dot(p.astype(bf16), pulled, NN)
                dkv_ref[at, :head] += dot(ds, query, NN) * scale
                part = dot(turned[:, at], ds, NN)
                mixed = part if mixed is None else mixed + part
            dq_ref[:, cols] = (mixed * scale).T.astype(bf16)

    block = min(rows_at_once, rows)
    return pl.pallas_call(
        kernel,
        out_shape=(
            jax.ShapeDtypeStruct((rows, heads * head), bf16),
            jax.ShapeDtypeStruct((keys, 2 * head), f32),
        ),
        grid=(rows // block,),
        in_specs=[pl.BlockSpec((block, heads * head), lambda i: (i, 0))]
        + [pl.BlockSpec((span, 2 * head), lambda i: (0, 0))] * count
        + [
            pl.BlockSpec((keys, 2), lambda i: (0, 0)),
            pl.BlockSpec((8, block), lambda i: (0, i)),
            pl.BlockSpec((8, block), lambda i: (0, i)),
            pl.BlockSpec((block, heads * head), lambda i: (i, 0)),
            pl.BlockSpec((block, heads * head), lambda i: (i, 0)),
        ],
        out_specs=(
            pl.BlockSpec((block, heads * head), lambda i: (i, 0)),
            pl.BlockSpec((keys, 2 * head), lambda i: (0, 0)),
        ),
        scratch_shapes=[
            pltpu.VMEM((head, keys), bf16),
        ],
        compiler_params=params(44),
        cost_estimate=cost(
            10 * rows * keys * heads * head, 8 * keys * head + 6 * rows * heads * head, rows * keys * heads
        ),
    )(qkv, *kv_blocks, key_info, query_info, logs, grad, out)


def parent_lookup(seg_ids, parents):
    labels = jnp.arange(parents.shape[0], dtype=jnp.int32)
    picked = jnp.where(seg_ids[:, None] == labels[None, :], parents[None, :], 0)
    return jnp.sum(picked, axis=1)


def gelu_parts(values):
    scale = math.sqrt(2.0 / math.pi)
    squared = values * values
    bend = jnp.tanh(scale * (values + 0.044715 * squared * values))
    out = 0.5 * values * (1.0 + bend)
    slope = 0.5 * (1.0 + bend) + 0.5 * values * (1.0 - bend * bend) * scale * (
        1.0 + 3 * 0.044715 * squared
    )
    return out, slope


def body(
    tokens,
    token_segment,
    segment_parent,
    ln1_gain,
    ln1_bias,
    q_weight,
    q_bias,
    kv_weight,
    value_bias,
    o_weight,
    o_bias,
    ln2_gain,
    ln2_bias,
    up_weight,
    up_bias,
    down_weight,
    down_bias,
    out_grad,
):
    row_count, width = tokens.shape
    head_size = value_bias.shape[0]
    local_width = q_weight.shape[1]
    local_heads = local_width // head_size
    tree_length = token_segment.shape[0]
    score_scale = 1.0 / math.sqrt(head_size)
    ctx_count = lax.axis_size("ctx")
    tp_count = lax.axis_size("tp")
    ctx_index = lax.axis_index("ctx")
    tp_index = lax.axis_index("tp")
    share_rows = row_count // tp_count
    ring = Ring(lax.axis_size("fsdp"), ctx_count, lax.axis_index("fsdp") * ctx_count + ctx_index)
    n = ring.size
    piece = width // n

    qkv_slots = ring.gather(jnp.concatenate([q_weight, kv_weight], axis=1), True)
    o_slots = ring.gather(o_weight, False)
    half = n // 2
    up_slots = ring.gather(up_weight, False, o_slots[1], o_slots[n - 1])
    down_slots = ring.gather(down_weight, True, up_slots[1], up_slots[n - 1])

    masks = [0]
    for bit in reversed(list(bits_of("tp"))):
        masks = masks + [m ^ bit for m in masks]
    row_blocks = [tp_index ^ m for m in masks]

    def rows_in(values):
        return jnp.concatenate(
            [
                lax.dynamic_slice_in_dim(values, b * share_rows, share_rows, 0)
                for b in row_blocks
            ],
            axis=0,
        )

    row_ids = jnp.stack(row_blocks)
    x_low_share, act_one = arrange(
        tokens, ln1_gain.astype(f32)[None], ln1_bias.astype(f32)[None], ring, row_ids
    )
    g_low = arrange(out_grad, None, None, ring, row_ids)
    vectors = ring.into(
        jnp.stack([ln1_gain, ln1_bias, o_bias, ln2_gain, ln2_bias, down_bias]).astype(f32)
    )
    gain_one, _, o_shift, gain_two, shift_two, down_shift = (
        vectors[i : i + 1] for i in range(6)
    )
    own_place = rows_in(jnp.arange(row_count, dtype=jnp.int32))

    parents = segment_parent[0]
    query_place = ctx_index * row_count + own_place
    key_places = []
    for d in range(ctx_count):
        start = (ctx_index - d) * row_count
        key_places.append(jnp.where(start >= 0, start + own_place, tree_length))
    key_place = jnp.concatenate(key_places)
    segment_blocks = rows_in(token_segment.reshape(ctx_count, row_count).T)
    own_seg = lax.dynamic_slice_in_dim(segment_blocks, ctx_index, 1, 1)[:, 0]
    key_segment = jnp.concatenate(
        [
            lax.dynamic_slice_in_dim(
                segment_blocks, lax.rem(ctx_index - d + ctx_count, ctx_count), 1, 1
            )[:, 0]
            for d in range(ctx_count)
        ]
    )
    seg_one = parent_lookup(own_seg, parents)
    seg_two = parent_lookup(seg_one, parents)
    key_info = jnp.stack([key_segment, key_place], axis=1)
    blank = jnp.zeros_like(own_seg)
    query_info = jnp.stack([own_seg, seg_one, seg_two, query_place, blank, blank, blank, blank])

    qkv_shift = jnp.concatenate(
        [q_bias.astype(f32), jnp.zeros((head_size,), f32), value_bias.astype(f32)]
    )

    def add_shift(total, extra, out, at):
        out[0][at, :] = (total + extra[0][...]).astype(bf16)

    (qkv,) = chunk_sum(
        act_one, qkv_slots, False, 256, [(qkv_shift[None], 1)], add_shift, [(bf16, row_count)]
    )
    kv_own = qkv[:, local_width:]
    kv_blocks = [kv_own] + [
        lax.ppermute(kv_own, "ctx", [(c, c + d) for c in range(ctx_count - d)])
        for d in range(1, ctx_count)
    ]
    attended, logs = attend(
        qkv, kv_blocks, key_info, query_info, local_heads, head_size, score_scale
    )
    attn_share = share_sum(*chunk_side(attended, o_slots, False))
    x_share = x_low_share.astype(f32)
    residual = x_share + (attn_share + o_shift)
    norm_two, inv_two = normed(residual)
    act_two = share_spread((norm_two * gain_two + shift_two).astype(bf16))


    def activate(total, extra, out, at):
        gelu_out, gelu_slope = gelu_parts(total + extra[0][...])
        out[0][at, :] = gelu_out.astype(bf16)
        out[1][at, :] = gelu_slope

    hidden, gelu_slope = chunk_sum(
        act_two,
        up_slots,
        False,
        512,
        [(up_bias.astype(f32)[None], 1)],
        activate,
        [(bf16, row_count), (f32, row_count)],
    )
    down_w_grad = ring.scatter(
        lambda k: dot(hidden, g_low[:, k * piece : (k + 1) * piece], TN), False
    )

    def deactivate(total, extra, out, at):
        low = (total * extra[0][at, :]).astype(bf16)
        out[0][at, :] = low
        summed = jnp.sum(low.astype(f32), axis=0, keepdims=True)
        out[1][...] = summed if at.start == 0 else out[1][...] + summed

    grad_pre, up_bias_grad = chunk_sum(
        g_low,
        down_slots,
        True,
        512,
        [(gelu_slope, row_count)],
        deactivate,
        [(bf16, row_count), (f32, 1)],
    )
    up_bias_grad = up_bias_grad[0]
    up_w_grad = ring.scatter(
        lambda k: dot(act_two[:, k * piece : (k + 1) * piece], grad_pre, TN), True
    )
    grad_two = share_sum(*chunk_side(grad_pre, up_slots, True))
    ffn_share = share_sum(*chunk_side(hidden, down_slots, False))
    layer_out = ring.back((residual + (ffn_share + down_shift)).astype(bf16))

    g_share = g_low[:share_rows].astype(f32)
    grad_res = g_share + normed_back(grad_two, gain_two, norm_two, inv_two)
    grad_attn_share = grad_res.astype(bf16)
    grad_attn = share_spread(grad_attn_share)
    out_w_grad = ring.scatter(
        lambda k: dot(attended, grad_attn[:, k * piece : (k + 1) * piece], TN), False
    )

    def only_round(total, extra, out, at):
        out[0][at, :] = total.astype(bf16)

    (grad_attended,) = chunk_sum(
        grad_attn, o_slots, True, 256, [], only_round, [(bf16, row_count)]
    )
    early = jnp.stack(
        [
            jnp.sum(g_share, axis=0),
            jnp.sum(grad_attn_share.astype(f32), axis=0),
            jnp.sum(grad_two * norm_two, axis=0),
            jnp.sum(grad_two, axis=0),
        ]
    )
    early = everyone_sum(ring.back(early).reshape(-1), ("tp",))

    grad_query, kv_grad = attend_back(
        qkv, kv_blocks, key_info, query_info, logs, grad_attended, attended,
        local_heads, head_size, score_scale,
    )
    q_bias_grad = jnp.sum(grad_query.astype(f32), axis=0)

    kv_part = kv_grad.astype(bf16).reshape(ctx_count, 2, row_count // 2, 2 * head_size)
    kv_part = share_sum(
        kv_part[:, 0].reshape(-1, 2 * head_size),
        kv_part[:, 1].reshape(-1, 2 * head_size),
        ctx_count,
    ).reshape(ctx_count, share_rows, 2 * head_size)
    kv_sum = kv_part[0]
    for d in range(1, ctx_count):
        kv_sum = kv_sum + lax.ppermute(
            kv_part[d].astype(bf16), "ctx", [(c, c - d) for c in range(d, ctx_count)]
        ).astype(f32)
    kv_low_share = kv_sum.astype(bf16)
    kv_low = share_spread(kv_low_share)

    sub = piece // tp_count

    def q_kv_part(k):
        act_piece = act_one[:, k * piece : (k + 1) * piece]
        q_piece = dot(act_piece, grad_query, TN)
        kv_piece = lax.dynamic_slice_in_dim(dot(act_piece, kv_low, TN), tp_index * sub, sub, 0)
        kv_piece = jnp.concatenate([kv_piece[: sub // 2], kv_piece[sub // 2 :]], axis=1)
        return jnp.concatenate([q_piece, kv_piece], axis=0)

    q_kv = ring.scatter(q_kv_part, True)()
    q_w_grad = q_kv[:piece]
    kv_w_grad = jnp.concatenate(
        [q_kv[piece:, : 2 * head_size], q_kv[piece:, 2 * head_size :]], axis=0
    )

    kv_full = jnp.concatenate([c[:, local_width:] for c in qkv_slots], axis=0)
    grad_act = share_sum(*chunk_side(grad_query, qkv_slots, True)) + dot(
        kv_low_share, kv_full, NT
    )
    norm_share, inv_share = normed(x_share)
    input_grad = ring.back(
        (grad_res + normed_back(grad_act, gain_one, norm_share, inv_share)).astype(bf16)
    )
    late = jnp.stack([jnp.sum(grad_act * norm_share, axis=0), jnp.sum(grad_act, axis=0)])
    late = ring.back(late).reshape(-1)
    value_bias_grad = jnp.sum(kv_low_share[:, head_size:].astype(f32), axis=0)
    late = everyone_sum(jnp.concatenate([late, value_bias_grad]), ("tp",))
    sums = [late, early, q_bias_grad, up_bias_grad]
    cuts = np.cumsum([v.shape[0] for v in sums])
    sums = everyone_sum(jnp.concatenate(sums), ("ctx", "fsdp"))
    late, early, q_bias_out, up_bias_out = (
        sums[stop - v.shape[0] : stop]
        for stop, v in zip(cuts, (late, early, q_bias_grad, up_bias_grad))
    )
    early = early.reshape(4, width)
    down_w_grad = down_w_grad(grad_query)
    up_w_grad = up_w_grad(grad_query)
    out_w_grad = out_w_grad(None)
    return (
        layer_out,
        input_grad,
        late[:width],
        late[width : 2 * width],
        q_w_grad,
        q_bias_out,
        kv_w_grad,
        late[2 * width :],
        out_w_grad,
        early[1],
        early[2],
        early[3],
        up_w_grad,
        up_bias_out,
        down_w_grad,
        early[0],
    )


def solution(mesh):
    whole = P()
    rows = P(("fsdp", "ctx"), None)
    split = P(("fsdp", "ctx"), "tp")
    turned = P("tp", ("fsdp", "ctx"))
    thin = P(("fsdp", "ctx", "tp"), None)
    in_specs = (
        rows, P("fsdp"), P("fsdp", None), whole, whole, split, P("tp"), rows, whole,
        turned, whole, whole, whole, split, P("tp"), turned, whole, rows,
    )
    out_specs = (
        thin, thin, whole, whole, split, P("tp"), thin, whole, turned, whole, whole, whole,
        split, P("tp"), turned, whole,
    )
    return jax.shard_map(body, mesh=mesh, in_specs=in_specs, out_specs=out_specs, check_vma=False)
```

```python
import math

import jax
import jax.numpy as jnp
import numpy as np
from jax import lax
from jax.experimental import pallas as pl
from jax.experimental.pallas import tpu as pltpu
from jax.sharding import PartitionSpec as P

eps = 1e-05
masked_score = -1000000000.0
log2_e = math.log2(math.e)
f32 = jnp.float32
bf16 = jnp.bfloat16
ring_axes = ("fsdp", "ctx")


def ring_order(rows, cols):
    if rows == 1:
        return list(range(cols))
    if cols == 1:
        return list(range(rows))
    if rows % 2 == 0:
        walk = [(0, c) for c in range(cols)]
        for step, c in enumerate(range(cols - 1, -1, -1)):
            span = range(1, rows) if step % 2 == 0 else range(rows - 1, 0, -1)
            walk += [(r, c) for r in span]
        if cols % 2 == 0 or rows == 2:
            return [r * cols + c for r, c in walk]
    return list(range(rows * cols))


def after(value, gate):
    if gate is None:
        return value
    return lax.optimization_barrier((value, gate))[0]


class Ring:
    def __init__(self, rows, cols, place):
        self.size = rows * cols
        order = ring_order(rows, cols)
        where = [0] * self.size
        for spot, owner in enumerate(order):
            where[owner] = spot
        n = self.size
        self.right = [(order[i], order[(i + 1) % n]) for i in range(n)]
        self.left = [(b, a) for a, b in self.right]
        spot = jnp.asarray(np.array(where, np.int32))[place]
        self.slots = jnp.asarray(np.array(order, np.int32))[
            lax.rem(spot - jnp.arange(n, dtype=jnp.int32) + n, n)
        ]
        self.homes = lax.rem(spot - jnp.asarray(np.array(where, np.int32)) + n, n)

    def hops(self, flip):
        far = self.size // 2
        near = self.size - 1 - far
        return (near, far) if flip else (far, near)

    def gather(self, shard, flip, gate_right=None, gate_left=None):
        hops_right, hops_left = self.hops(flip)
        slots = [shard] * self.size
        moving = after(shard, gate_right)
        for k in range(1, hops_right + 1):
            moving = lax.ppermute(moving, ring_axes, self.right)
            slots[k] = moving
        moving = after(shard, gate_left)
        for k in range(1, hops_left + 1):
            moving = lax.ppermute(moving, ring_axes, self.left)
            slots[self.size - k] = moving
        return slots

    def scatter(self, part, flip, early=None):
        hops_right, hops_left = self.hops(flip)
        n = self.size
        last = []
        legs = []
        for hops, sign, pairs in ((hops_right, -1, self.right), (hops_left, 1, self.left)):
            if hops:
                legs.append([hops, sign, pairs, None])

        def run(stop, gate=None):
            for leg in legs:
                while leg[0] > stop(leg):
                    hops, sign, pairs, moving = leg
                    piece = part((sign * hops) % n)
                    if moving is not None:
                        if gate is not None:
                            moving = after(moving, gate)
                        piece = piece + moving.astype(f32)
                    leg[3] = lax.ppermute(piece.astype(bf16), ring_axes, pairs)
                    leg[0] = hops - 1

        if early is None:
            run(lambda leg: 0)
        else:
            begin = [leg[0] for leg in legs]
            run(lambda leg: begin[legs.index(leg)] - early)

        def resume(gate):
            run(lambda leg: 0, gate)

        def finish(gate=None):
            total = part(0)
            for leg in legs:
                total = total + after(leg[3], gate).astype(f32)
            return total

        return finish if early is None else (finish, resume)

    def into(self, values):
        width = values.shape[-1] // self.size
        return jnp.concatenate(
            [
                lax.dynamic_slice_in_dim(values, self.slots[k] * width, width, values.ndim - 1)
                for k in range(self.size)
            ],
            axis=-1,
        )

    def back(self, values):
        width = values.shape[-1] // self.size
        return jnp.concatenate(
            [
                lax.dynamic_slice_in_dim(values, self.homes[k] * width, width, values.ndim - 1)
                for k in range(self.size)
            ],
            axis=-1,
        )


def swap(values, axis, bit):
    count = lax.axis_size(axis)
    return lax.ppermute(values, axis, [(i, i ^ bit) for i in range(count)])


def bits_of(axis):
    count = lax.axis_size(axis)
    bit = 1
    while bit < count:
        yield bit
        bit *= 2


def share_sum(keep, send, groups=1):
    width = keep.shape[-1]
    for bit in bits_of("tp"):
        total = keep.astype(f32) + swap(send, "tp", bit).astype(f32)
        if 2 * bit == lax.axis_size("tp"):
            return total
        halves = total.reshape(groups, 2, -1, width)
        keep = halves[:, 0].reshape(-1, width)
        send = halves[:, 1].reshape(-1, width).astype(bf16)


def share_spread(rows):
    for bit in reversed(list(bits_of("tp"))):
        rows = jnp.concatenate([rows, swap(rows, "tp", bit)], axis=0)
    return rows


def everyone_sum(values, axes):
    for axis in axes:
        for bit in bits_of(axis):
            values = values + swap(values, axis, bit)
    return values


def dot(left, right, dims):
    return lax.dot_general(left, right, (dims, ((), ())), preferred_element_type=f32)


NN = ((1,), (0,))
NT = ((1,), (1,))
TN = ((0,), (0,))


def normed(values):
    center = jnp.mean(values, axis=-1, keepdims=True)
    centred = values - center
    spread = jnp.mean(centred * centred, axis=-1, keepdims=True)
    inv = lax.rsqrt(spread + eps)
    return centred * inv, inv


def normed_back(grad, gain, norm, inv):
    pulled = grad * gain
    term = pulled - jnp.mean(pulled, axis=-1, keepdims=True)
    return inv * (term - norm * jnp.mean(pulled * norm, axis=-1, keepdims=True))


def params(megabytes):
    return pltpu.CompilerParams(vmem_limit_bytes=megabytes << 20)


def cost(flops, moved, heavy=0):
    return pl.CostEstimate(flops=flops, bytes_accessed=moved, transcendentals=heavy)


def arrange(values, gain, shift, ring, row_blocks):
    rows, width = values.shape
    blocks = row_blocks.shape[0]
    pieces = ring.size
    share = rows // blocks
    piece = width // pieces
    norm = gain is not None
    moved = piece % 128 == 0
    if not moved:
        values = ring.into(values)
        if norm:
            gain, shift = ring.into(gain), ring.into(shift)

    def source(slot_ref, k):
        if not moved:
            return slice(k * piece, (k + 1) * piece)
        return pl.ds(pl.multiple_of(slot_ref[k] * piece, piece), piece)

    def kernel(slot_ref, block_ref, *refs):
        del block_ref
        if norm:
            in_ref, gain_ref, shift_ref, share_ref, act_ref, natural = refs
        else:
            in_ref, share_ref = refs
        for k in range(pieces):
            from_cols = source(slot_ref, k)
            cols = slice(k * piece, (k + 1) * piece)
            if norm:
                @pl.when(pl.program_id(0) == 0)
                def _(cols=cols, from_cols=from_cols):
                    share_ref[:, cols] = in_ref[:, from_cols]
            else:
                share_ref[:, cols] = in_ref[:, from_cols]
        if norm:
            unit, _ = normed(in_ref[...].astype(f32))
            natural[...] = (unit * gain_ref[...] + shift_ref[...]).astype(bf16)
            for k in range(pieces):
                from_cols = source(slot_ref, k)
                act_ref[:, k * piece : (k + 1) * piece] = natural[:, from_cols]

    row_in = pl.BlockSpec((share, width), lambda i, s, b: (b[i], 0))
    row_out = pl.BlockSpec((share, width), lambda i, s, b: (i, 0))
    first = pl.BlockSpec((share, width), lambda i, s, b: (0, 0))
    line = pl.BlockSpec((1, width), lambda i, s, b: (0, 0))
    full = jax.ShapeDtypeStruct((rows, width), bf16)
    return pl.pallas_call(
        kernel,
        out_shape=(jax.ShapeDtypeStruct((share, width), bf16), full) if norm else full,
        grid_spec=pltpu.PrefetchScalarGridSpec(
            num_scalar_prefetch=2,
            grid=(blocks,),
            in_specs=[row_in, line, line] if norm else [row_in],
            out_specs=(first, row_out) if norm else row_out,
            scratch_shapes=[pltpu.VMEM((share, width), bf16)] if norm else [],
        ),
        compiler_params=params(24),
        cost_estimate=cost(10 * rows * width, 4 * rows * width),
    )(ring.slots, row_blocks, values, *((gain, shift) if norm else ()))


def slot_list(chunks, axis):
    if chunks[0].shape[axis] % 128 != 0:
        return [jnp.concatenate(chunks, axis=axis)]
    return chunks


def chunk_sum(left, chunks, turned, tile, extras, finish, outs, megabytes=40):
    chunks = slot_list(chunks, 1 if turned else 0)
    rows, depth = left.shape
    count = len(chunks)
    piece = depth // count
    columns = chunks[0].shape[0 if turned else 1]
    tile = min(tile, columns)

    def kernel(*refs):
        left_ref = refs[0]
        chunk_refs = refs[1 : 1 + count]
        extra_refs = refs[1 + count : 1 + count + len(extras)]
        out_refs = refs[1 + count + len(extras) :]
        step = min(rows, 256)
        for start in range(0, rows, step):
            at = slice(start, start + step)
            total = None
            for k in range(count):
                part = dot(
                    left_ref[at, k * piece : (k + 1) * piece],
                    chunk_refs[k][...],
                    NT if turned else NN,
                )
                total = part if total is None else total + part
            finish(total, extra_refs, out_refs, at)

    if turned:
        chunk_spec = pl.BlockSpec((tile, piece), lambda i: (i, 0))
    else:
        chunk_spec = pl.BlockSpec((piece, tile), lambda i: (0, i))
    return pl.pallas_call(
        kernel,
        out_shape=tuple(jax.ShapeDtypeStruct((r, columns), d) for d, r in outs),
        grid=(columns // tile,),
        in_specs=[pl.BlockSpec((rows, depth), lambda i: (0, 0))]
        + [chunk_spec] * count
        + [pl.BlockSpec((r, tile), lambda i: (0, i)) for _, r in extras],
        out_specs=tuple(pl.BlockSpec((r, tile), lambda i: (0, i)) for _, r in outs),
        compiler_params=params(megabytes),
        cost_estimate=cost(
            2 * rows * depth * columns, 2 * (rows * depth + depth * columns) + 8 * rows * columns
        ),
    )(left, *chunks, *(a for a, _ in extras))


def chunk_side(left, chunks, turned, megabytes=40):
    chunks = slot_list(chunks, 0 if turned else 1)
    rows, depth = left.shape
    count = len(chunks)
    piece = chunks[0].shape[0 if turned else 1]
    block = (piece, depth) if turned else (depth, piece)
    half = rows // 2

    def kernel(*refs):
        left_ref = refs[0]
        chunk_refs = refs[1 : 1 + count]
        keep_ref, send_ref, held, sems = refs[1 + count :]
        def copy(k):
            source = chunk_refs[k]
            if chunk_refs[k].shape != block:
                source = source.at[:, :depth] if turned else source.at[:depth, :]
            return pltpu.make_async_copy(source, held.at[k], sems.at[k])
        for k in range(count):
            copy(k).start()
        for k in range(count):
            copy(k).wait()
            for out_ref, start in ((keep_ref, 0), (send_ref, half)):
                part = dot(left_ref[start : start + half, :], held[k], NT if turned else NN)
                out_ref[:, k * piece : (k + 1) * piece] = part.astype(bf16)

    shape = jax.ShapeDtypeStruct((half, piece * count), bf16)
    return pl.pallas_call(
        kernel,
        out_shape=(shape, shape),
        in_specs=[pl.BlockSpec(memory_space=pltpu.VMEM)]
        + [pl.BlockSpec(memory_space=pl.ANY)] * count,
        out_specs=(pl.BlockSpec(memory_space=pltpu.VMEM),) * 2,
        scratch_shapes=[pltpu.VMEM((count,) + block, bf16), pltpu.SemaphoreType.DMA((count,))],
        compiler_params=params(megabytes),
        cost_estimate=cost(
            2 * rows * depth * piece * count,
            2 * (rows * depth + depth * piece * count + rows * piece * count),
        ),
    )(left, *chunks)


def mask_of(info_ref, key_ref, keys):
    own, one, two, place = (info_ref[i : i + 1, :] for i in range(4))
    seg = key_ref[keys, 0:1]
    spot = key_ref[keys, 1:2]
    return ((seg == own) | (seg == one) | (seg == two)) & (spot <= place)


def attend(qkv, kv_blocks, key_info, query_info, heads, head, scale, rows_at_once=512):
    rows = qkv.shape[0]
    count = len(kv_blocks)
    span = kv_blocks[0].shape[0]
    keys = span * count

    def kernel(q_ref, *refs):
        kv_refs = refs[:count]
        key_ref, info_ref, out_ref, log_ref, turned, score = refs[count:]

        @pl.when(pl.program_id(0) == 0)
        def _():
            for d in range(count):
                turned[:, d * span : (d + 1) * span] = kv_refs[d][:, head:].T

        masks = [
            mask_of(info_ref, key_ref, slice(d * span, (d + 1) * span)) for d in range(count)
        ]
        for h in range(heads):
            query = q_ref[:, h * head : (h + 1) * head]
            top = None
            for d in range(count):
                raw = dot(kv_refs[d][:, :head], query, NT)
                raw = jnp.where(masks[d], raw, masked_score / scale)
                score[d * span : (d + 1) * span, :] = raw
                peak = jnp.max(raw, axis=0, keepdims=True)
                top = peak if top is None else jnp.maximum(top, peak)
            total = mixed = None
            for d in range(count):
                e = jnp.exp2((score[d * span : (d + 1) * span, :] - top) * (scale * log2_e))
                summed = jnp.sum(e, axis=0, keepdims=True)
                total = summed if total is None else total + summed
                part = dot(turned[:, d * span : (d + 1) * span], e.astype(bf16), NN)
                mixed = part if mixed is None else mixed + part
            out_ref[:, h * head : (h + 1) * head] = (mixed * (1.0 / total)).T.astype(bf16)
            log_ref[h : h + 1, :] = (top * scale + jnp.log(total)) * log2_e

    block = min(rows_at_once, rows)
    return pl.pallas_call(
        kernel,
        out_shape=(
            jax.ShapeDtypeStruct((rows, heads * head), bf16),
            jax.ShapeDtypeStruct((8, rows), f32),
        ),
        grid=(rows // block,),
        in_specs=[pl.BlockSpec((block, heads * head), lambda i: (i, 0))]
        + [pl.BlockSpec((span, 2 * head), lambda i: (0, 0))] * count
        + [
            pl.BlockSpec((keys, 2), lambda i: (0, 0)),
            pl.BlockSpec((8, block), lambda i: (0, i)),
        ],
        out_specs=(
            pl.BlockSpec((block, heads * head), lambda i: (i, 0)),
            pl.BlockSpec((8, block), lambda i: (0, i)),
        ),
        scratch_shapes=[
            pltpu.VMEM((head, keys), bf16),
            pltpu.VMEM((keys, block), f32),
        ],
        compiler_params=params(40),
        cost_estimate=cost(4 * rows * keys * heads * head, 4 * rows * heads * head, rows * keys * heads),
    )(qkv, *kv_blocks, key_info, query_info)


def attend_back(qkv, kv_blocks, key_info, query_info, logs, grad, out, heads, head, scale, rows_at_once=256):
    rows = qkv.shape[0]
    count = len(kv_blocks)
    span = kv_blocks[0].shape[0]
    keys = span * count

    def kernel(q_ref, *refs):
        kv_refs = refs[:count]
        key_ref, info_ref, log_ref, grad_ref, out_ref, dq_ref, dkv_ref, turned = refs[count:]

        @pl.when(pl.program_id(0) == 0)
        def _():
            for d in range(count):
                turned[:, d * span : (d + 1) * span] = kv_refs[d][:, :head].T
            dkv_ref[...] = jnp.zeros_like(dkv_ref)

        masks = [
            mask_of(info_ref, key_ref, slice(d * span, (d + 1) * span)) for d in range(count)
        ]
        for h in range(heads):
            cols = slice(h * head, (h + 1) * head)
            query = q_ref[:, cols]
            pulled = grad_ref[:, cols]
            log = log_ref[h : h + 1, :]
            delta = jnp.sum(
                (pulled.astype(f32) * out_ref[:, cols].astype(f32)).T, axis=0, keepdims=True
            )
            mixed = None
            for d in range(count):
                at = slice(d * span, (d + 1) * span)
                raw = dot(kv_refs[d][:, :head], query, NT) * (scale * log2_e)
                p = jnp.exp2(jnp.where(masks[d], raw, masked_score) - log)
                g = dot(kv_refs[d][:, head:], pulled, NT)
                ds = (p * (g - delta)).astype(bf16)
                dkv_ref[at, head:] += dot(p.astype(bf16), pulled, NN)
                dkv_ref[at, :head] += dot(ds, query, NN) * scale
                part = dot(turned[:, at], ds, NN)
                mixed = part if mixed is None else mixed + part
            dq_ref[:, cols] = (mixed * scale).T.astype(bf16)

    block = min(rows_at_once, rows)
    return pl.pallas_call(
        kernel,
        out_shape=(
            jax.ShapeDtypeStruct((rows, heads * head), bf16),
            jax.ShapeDtypeStruct((keys, 2 * head), f32),
        ),
        grid=(rows // block,),
        in_specs=[pl.BlockSpec((block, heads * head), lambda i: (i, 0))]
        + [pl.BlockSpec((span, 2 * head), lambda i: (0, 0))] * count
        + [
            pl.BlockSpec((keys, 2), lambda i: (0, 0)),
            pl.BlockSpec((8, block), lambda i: (0, i)),
            pl.BlockSpec((8, block), lambda i: (0, i)),
            pl.BlockSpec((block, heads * head), lambda i: (i, 0)),
            pl.BlockSpec((block, heads * head), lambda i: (i, 0)),
        ],
        out_specs=(
            pl.BlockSpec((block, heads * head), lambda i: (i, 0)),
            pl.BlockSpec((keys, 2 * head), lambda i: (0, 0)),
        ),
        scratch_shapes=[
            pltpu.VMEM((head, keys), bf16),
        ],
        compiler_params=params(44),
        cost_estimate=cost(
            10 * rows * keys * heads * head, 8 * keys * head + 6 * rows * heads * head, rows * keys * heads
        ),
    )(qkv, *kv_blocks, key_info, query_info, logs, grad, out)


def parent_lookup(seg_ids, parents):
    labels = jnp.arange(parents.shape[0], dtype=jnp.int32)
    picked = jnp.where(seg_ids[:, None] == labels[None, :], parents[None, :], 0)
    return jnp.sum(picked, axis=1)


def gelu_parts(values):
    scale = math.sqrt(2.0 / math.pi)
    squared = values * values
    bend = jnp.tanh(scale * (values + 0.044715 * squared * values))
    out = 0.5 * values * (1.0 + bend)
    slope = 0.5 * (1.0 + bend) + 0.5 * values * (1.0 - bend * bend) * scale * (
        1.0 + 3 * 0.044715 * squared
    )
    return out, slope


def body(
    tokens,
    token_segment,
    segment_parent,
    ln1_gain,
    ln1_bias,
    q_weight,
    q_bias,
    kv_weight,
    value_bias,
    o_weight,
    o_bias,
    ln2_gain,
    ln2_bias,
    up_weight,
    up_bias,
    down_weight,
    down_bias,
    out_grad,
):
    row_count, width = tokens.shape
    head_size = value_bias.shape[0]
    local_width = q_weight.shape[1]
    local_heads = local_width // head_size
    tree_length = token_segment.shape[0]
    score_scale = 1.0 / math.sqrt(head_size)
    ctx_count = lax.axis_size("ctx")
    tp_count = lax.axis_size("tp")
    ctx_index = lax.axis_index("ctx")
    tp_index = lax.axis_index("tp")
    share_rows = row_count // tp_count
    ring = Ring(lax.axis_size("fsdp"), ctx_count, lax.axis_index("fsdp") * ctx_count + ctx_index)
    n = ring.size
    piece = width // n

    qkv_slots = ring.gather(jnp.concatenate([q_weight, kv_weight], axis=1), True)
    o_slots = ring.gather(o_weight, False)
    half = n // 2
    up_slots = ring.gather(up_weight, False, o_slots[1], o_slots[n - 1])
    down_slots = ring.gather(down_weight, True, up_slots[1], up_slots[n - 1])

    masks = [0]
    for bit in reversed(list(bits_of("tp"))):
        masks = masks + [m ^ bit for m in masks]
    row_blocks = [tp_index ^ m for m in masks]

    def rows_in(values):
        return jnp.concatenate(
            [
                lax.dynamic_slice_in_dim(values, b * share_rows, share_rows, 0)
                for b in row_blocks
            ],
            axis=0,
        )

    row_ids = jnp.stack(row_blocks)
    x_low_share, act_one = arrange(
        tokens, ln1_gain.astype(f32)[None], ln1_bias.astype(f32)[None], ring, row_ids
    )
    g_low = arrange(out_grad, None, None, ring, row_ids)
    vectors = ring.into(
        jnp.stack([ln1_gain, ln1_bias, o_bias, ln2_gain, ln2_bias, down_bias]).astype(f32)
    )
    gain_one, _, o_shift, gain_two, shift_two, down_shift = (
        vectors[i : i + 1] for i in range(6)
    )
    own_place = rows_in(jnp.arange(row_count, dtype=jnp.int32))

    parents = segment_parent[0]
    query_place = ctx_index * row_count + own_place
    key_places = []
    for d in range(ctx_count):
        start = (ctx_index - d) * row_count
        key_places.append(jnp.where(start >= 0, start + own_place, tree_length))
    key_place = jnp.concatenate(key_places)
    segment_blocks = rows_in(token_segment.reshape(ctx_count, row_count).T)
    own_seg = lax.dynamic_slice_in_dim(segment_blocks, ctx_index, 1, 1)[:, 0]
    key_segment = jnp.concatenate(
        [
            lax.dynamic_slice_in_dim(
                segment_blocks, lax.rem(ctx_index - d + ctx_count, ctx_count), 1, 1
            )[:, 0]
            for d in range(ctx_count)
        ]
    )
    seg_one = parent_lookup(own_seg, parents)
    seg_two = parent_lookup(seg_one, parents)
    key_info = jnp.stack([key_segment, key_place], axis=1)
    blank = jnp.zeros_like(own_seg)
    query_info = jnp.stack([own_seg, seg_one, seg_two, query_place, blank, blank, blank, blank])

    qkv_shift = jnp.concatenate(
        [q_bias.astype(f32), jnp.zeros((head_size,), f32), value_bias.astype(f32)]
    )

    def add_shift(total, extra, out, at):
        out[0][at, :] = (total + extra[0][...]).astype(bf16)

    (qkv,) = chunk_sum(
        act_one, qkv_slots, False, 256, [(qkv_shift[None], 1)], add_shift, [(bf16, row_count)]
    )
    kv_own = qkv[:, local_width:]
    kv_blocks = [kv_own] + [
        lax.ppermute(kv_own, "ctx", [(c, c + d) for c in range(ctx_count - d)])
        for d in range(1, ctx_count)
    ]
    attended, logs = attend(
        qkv, kv_blocks, key_info, query_info, local_heads, head_size, score_scale
    )
    attn_share = share_sum(*chunk_side(attended, o_slots, False))
    x_share = x_low_share.astype(f32)
    residual = x_share + (attn_share + o_shift)
    norm_two, inv_two = normed(residual)
    act_two = share_spread((norm_two * gain_two + shift_two).astype(bf16))


    def activate(total, extra, out, at):
        gelu_out, gelu_slope = gelu_parts(total + extra[0][...])
        out[0][at, :] = gelu_out.astype(bf16)
        out[1][at, :] = gelu_slope

    hidden, gelu_slope = chunk_sum(
        act_two,
        up_slots,
        False,
        512,
        [(up_bias.astype(f32)[None], 1)],
        activate,
        [(bf16, row_count), (f32, row_count)],
    )
    down_w_grad = ring.scatter(
        lambda k: dot(hidden, g_low[:, k * piece : (k + 1) * piece], TN), False
    )

    def deactivate(total, extra, out, at):
        low = (total * extra[0][at, :]).astype(bf16)
        out[0][at, :] = low
        summed = jnp.sum(low.astype(f32), axis=0, keepdims=True)
        out[1][...] = summed if at.start == 0 else out[1][...] + summed

    grad_pre, up_bias_grad = chunk_sum(
        g_low,
        down_slots,
        True,
        512,
        [(gelu_slope, row_count)],
        deactivate,
        [(bf16, row_count), (f32, 1)],
    )
    up_bias_grad = up_bias_grad[0]
    up_w_grad = ring.scatter(
        lambda k: dot(act_two[:, k * piece : (k + 1) * piece], grad_pre, TN), True
    )
    grad_two = share_sum(*chunk_side(grad_pre, up_slots, True))

    g_share = g_low[:share_rows].astype(f32)
    grad_res = g_share + normed_back(grad_two, gain_two, norm_two, inv_two)
    grad_attn_share = grad_res.astype(bf16)
    grad_attn = share_spread(grad_attn_share)
    out_w_grad, out_resume = ring.scatter(
        lambda k: dot(attended, grad_attn[:, k * piece : (k + 1) * piece], TN), False, 1
    )

    def only_round(total, extra, out, at):
        out[0][at, :] = total.astype(bf16)

    (grad_attended,) = chunk_sum(
        grad_attn, o_slots, True, 256, [], only_round, [(bf16, row_count)]
    )
    ffn_share = share_sum(*chunk_side(after(hidden, grad_attended), down_slots, False))
    layer_out = ring.back((residual + (ffn_share + down_shift)).astype(bf16))
    early = jnp.stack(
        [
            jnp.sum(g_share, axis=0),
            jnp.sum(grad_attn_share.astype(f32), axis=0),
            jnp.sum(grad_two * norm_two, axis=0),
            jnp.sum(grad_two, axis=0),
        ]
    )
    early = ring.back(early).reshape(-1)

    grad_query, kv_grad = attend_back(
        qkv, kv_blocks, key_info, query_info, logs, grad_attended, attended,
        local_heads, head_size, score_scale,
    )
    q_bias_grad = jnp.sum(grad_query.astype(f32), axis=0)

    kv_part = kv_grad.astype(bf16).reshape(ctx_count, 2, row_count // 2, 2 * head_size)
    kv_part = share_sum(
        kv_part[:, 0].reshape(-1, 2 * head_size),
        kv_part[:, 1].reshape(-1, 2 * head_size),
        ctx_count,
    ).reshape(ctx_count, share_rows, 2 * head_size)
    kv_sum = kv_part[0]
    for d in range(1, ctx_count):
        kv_sum = kv_sum + lax.ppermute(
            kv_part[d].astype(bf16), "ctx", [(c, c - d) for c in range(d, ctx_count)]
        ).astype(f32)
    kv_low_share = kv_sum.astype(bf16)
    kv_low = share_spread(kv_low_share)
    out_resume(kv_low)

    sub = piece // tp_count

    def q_kv_part(k):
        act_piece = act_one[:, k * piece : (k + 1) * piece]
        q_piece = dot(act_piece, grad_query, TN)
        kv_piece = lax.dynamic_slice_in_dim(dot(act_piece, kv_low, TN), tp_index * sub, sub, 0)
        kv_piece = jnp.concatenate([kv_piece[: sub // 2], kv_piece[sub // 2 :]], axis=1)
        return jnp.concatenate([q_piece, kv_piece], axis=0)

    q_kv = ring.scatter(q_kv_part, True)()
    q_w_grad = q_kv[:piece]
    kv_w_grad = jnp.concatenate(
        [q_kv[piece:, : 2 * head_size], q_kv[piece:, 2 * head_size :]], axis=0
    )

    kv_full = jnp.concatenate([c[:, local_width:] for c in qkv_slots], axis=0)
    grad_act = share_sum(*chunk_side(grad_query, qkv_slots, True)) + dot(
        kv_low_share, kv_full, NT
    )
    norm_share, inv_share = normed(x_share)
    input_grad = ring.back(
        (grad_res + normed_back(grad_act, gain_one, norm_share, inv_share)).astype(bf16)
    )
    late = jnp.stack([jnp.sum(grad_act * norm_share, axis=0), jnp.sum(grad_act, axis=0)])
    late = ring.back(late).reshape(-1)
    value_bias_grad = jnp.sum(kv_low_share[:, head_size:].astype(f32), axis=0)
    late = everyone_sum(jnp.concatenate([late, value_bias_grad, early]), ("tp",))
    early = late[2 * width + head_size :]
    late = late[: 2 * width + head_size]
    sums = [late, early, q_bias_grad, up_bias_grad]
    cuts = np.cumsum([v.shape[0] for v in sums])
    sums = everyone_sum(jnp.concatenate(sums), ("ctx", "fsdp"))
    late, early, q_bias_out, up_bias_out = (
        sums[stop - v.shape[0] : stop]
        for stop, v in zip(cuts, (late, early, q_bias_grad, up_bias_grad))
    )
    early = early.reshape(4, width)
    down_w_grad = down_w_grad(grad_query)
    up_w_grad = up_w_grad(grad_query)
    out_w_grad = out_w_grad(None)
    return (
        layer_out,
        input_grad,
        late[:width],
        late[width : 2 * width],
        q_w_grad,
        q_bias_out,
        kv_w_grad,
        late[2 * width :],
        out_w_grad,
        early[1],
        early[2],
        early[3],
        up_w_grad,
        up_bias_out,
        down_w_grad,
        early[0],
    )


def solution(mesh):
    whole = P()
    rows = P(("fsdp", "ctx"), None)
    split = P(("fsdp", "ctx"), "tp")
    turned = P("tp", ("fsdp", "ctx"))
    thin = P(("fsdp", "ctx", "tp"), None)
    in_specs = (
        rows, P("fsdp"), P("fsdp", None), whole, whole, split, P("tp"), rows, whole,
        turned, whole, whole, whole, split, P("tp"), turned, whole, rows,
    )
    out_specs = (
        thin, thin, whole, whole, split, P("tp"), thin, whole, turned, whole, whole, whole,
        split, P("tp"), turned, whole,
    )
    return jax.shard_map(body, mesh=mesh, in_specs=in_specs, out_specs=out_specs, check_vma=False)
```

```python
import math

import jax
import jax.numpy as jnp
import numpy as np
from jax import lax
from jax.experimental import pallas as pl
from jax.experimental.pallas import tpu as pltpu
from jax.sharding import PartitionSpec as P

eps = 1e-05
masked_score = -1000000000.0
log2_e = math.log2(math.e)
f32 = jnp.float32
bf16 = jnp.bfloat16
ring_axes = ("fsdp", "ctx")


def ring_order(rows, cols):
    if rows == 1:
        return list(range(cols))
    if cols == 1:
        return list(range(rows))
    if rows % 2 == 0:
        walk = [(0, c) for c in range(cols)]
        for step, c in enumerate(range(cols - 1, -1, -1)):
            span = range(1, rows) if step % 2 == 0 else range(rows - 1, 0, -1)
            walk += [(r, c) for r in span]
        if cols % 2 == 0 or rows == 2:
            return [r * cols + c for r, c in walk]
    return list(range(rows * cols))


def after(value, gate):
    if gate is None:
        return value
    return lax.optimization_barrier((value, gate))[0]


class Ring:
    def __init__(self, rows, cols, place):
        self.size = rows * cols
        order = ring_order(rows, cols)
        where = [0] * self.size
        for spot, owner in enumerate(order):
            where[owner] = spot
        n = self.size
        self.right = [(order[i], order[(i + 1) % n]) for i in range(n)]
        self.left = [(b, a) for a, b in self.right]
        spot = jnp.asarray(np.array(where, np.int32))[place]
        self.slots = jnp.asarray(np.array(order, np.int32))[
            lax.rem(spot - jnp.arange(n, dtype=jnp.int32) + n, n)
        ]
        self.homes = lax.rem(spot - jnp.asarray(np.array(where, np.int32)) + n, n)

    def hops(self, flip):
        far = self.size // 2
        near = self.size - 1 - far
        return (near, far) if flip else (far, near)

    def gather(self, shard, flip, gate_right=None, gate_left=None):
        hops_right, hops_left = self.hops(flip)
        slots = [shard] * self.size
        moving = after(shard, gate_right)
        for k in range(1, hops_right + 1):
            moving = lax.ppermute(moving, ring_axes, self.right)
            slots[k] = moving
        moving = after(shard, gate_left)
        for k in range(1, hops_left + 1):
            moving = lax.ppermute(moving, ring_axes, self.left)
            slots[self.size - k] = moving
        return slots

    def scatter(self, part, flip, early=None):
        hops_right, hops_left = self.hops(flip)
        n = self.size
        last = []
        legs = []
        for hops, sign, pairs in ((hops_right, -1, self.right), (hops_left, 1, self.left)):
            if hops:
                legs.append([hops, sign, pairs, None])

        def run(stop, gate=None):
            for leg in legs:
                while leg[0] > stop(leg):
                    hops, sign, pairs, moving = leg
                    piece = part((sign * hops) % n)
                    if moving is not None:
                        if gate is not None:
                            moving = after(moving, gate)
                        piece = piece + moving.astype(f32)
                    leg[3] = lax.ppermute(piece.astype(bf16), ring_axes, pairs)
                    leg[0] = hops - 1

        if early is None:
            run(lambda leg: 0)
        else:
            begin = [leg[0] for leg in legs]
            run(lambda leg: begin[legs.index(leg)] - early)

        def resume(gate):
            run(lambda leg: 0, gate)

        def finish(gate=None):
            total = part(0)
            for leg in legs:
                total = total + after(leg[3], gate).astype(f32)
            return total

        return finish if early is None else (finish, resume)

    def into(self, values):
        width = values.shape[-1] // self.size
        return jnp.concatenate(
            [
                lax.dynamic_slice_in_dim(values, self.slots[k] * width, width, values.ndim - 1)
                for k in range(self.size)
            ],
            axis=-1,
        )

    def back(self, values):
        width = values.shape[-1] // self.size
        return jnp.concatenate(
            [
                lax.dynamic_slice_in_dim(values, self.homes[k] * width, width, values.ndim - 1)
                for k in range(self.size)
            ],
            axis=-1,
        )


def swap(values, axis, bit):
    count = lax.axis_size(axis)
    return lax.ppermute(values, axis, [(i, i ^ bit) for i in range(count)])


def bits_of(axis):
    count = lax.axis_size(axis)
    bit = 1
    while bit < count:
        yield bit
        bit *= 2


def share_sum(keep, send, groups=1):
    width = keep.shape[-1]
    for bit in bits_of("tp"):
        total = keep.astype(f32) + swap(send, "tp", bit).astype(f32)
        if 2 * bit == lax.axis_size("tp"):
            return total
        halves = total.reshape(groups, 2, -1, width)
        keep = halves[:, 0].reshape(-1, width)
        send = halves[:, 1].reshape(-1, width).astype(bf16)


def share_spread(rows):
    for bit in reversed(list(bits_of("tp"))):
        rows = jnp.concatenate([rows, swap(rows, "tp", bit)], axis=0)
    return rows


def everyone_sum(values, axes):
    for axis in axes:
        for bit in bits_of(axis):
            values = values + swap(values, axis, bit)
    return values


def dot(left, right, dims):
    return lax.dot_general(left, right, (dims, ((), ())), preferred_element_type=f32)


NN = ((1,), (0,))
NT = ((1,), (1,))
TN = ((0,), (0,))


def normed(values):
    center = jnp.mean(values, axis=-1, keepdims=True)
    centred = values - center
    spread = jnp.mean(centred * centred, axis=-1, keepdims=True)
    inv = lax.rsqrt(spread + eps)
    return centred * inv, inv


def normed_back(grad, gain, norm, inv):
    pulled = grad * gain
    term = pulled - jnp.mean(pulled, axis=-1, keepdims=True)
    return inv * (term - norm * jnp.mean(pulled * norm, axis=-1, keepdims=True))


def params(megabytes):
    return pltpu.CompilerParams(vmem_limit_bytes=megabytes << 20)


def cost(flops, moved, heavy=0):
    return pl.CostEstimate(flops=flops, bytes_accessed=moved, transcendentals=heavy)


def arrange(values, gain, shift, ring, row_blocks):
    rows, width = values.shape
    blocks = row_blocks.shape[0]
    pieces = ring.size
    share = rows // blocks
    piece = width // pieces
    norm = gain is not None
    moved = piece % 128 == 0
    if not moved:
        values = ring.into(values)
        if norm:
            gain, shift = ring.into(gain), ring.into(shift)

    def source(slot_ref, k):
        if not moved:
            return slice(k * piece, (k + 1) * piece)
        return pl.ds(pl.multiple_of(slot_ref[k] * piece, piece), piece)

    def kernel(slot_ref, block_ref, *refs):
        del block_ref
        if norm:
            in_ref, gain_ref, shift_ref, share_ref, act_ref, natural = refs
        else:
            in_ref, share_ref = refs
        for k in range(pieces):
            from_cols = source(slot_ref, k)
            cols = slice(k * piece, (k + 1) * piece)
            if norm:
                @pl.when(pl.program_id(0) == 0)
                def _(cols=cols, from_cols=from_cols):
                    share_ref[:, cols] = in_ref[:, from_cols]
            else:
                share_ref[:, cols] = in_ref[:, from_cols]
        if norm:
            unit, _ = normed(in_ref[...].astype(f32))
            natural[...] = (unit * gain_ref[...] + shift_ref[...]).astype(bf16)
            for k in range(pieces):
                from_cols = source(slot_ref, k)
                act_ref[:, k * piece : (k + 1) * piece] = natural[:, from_cols]

    row_in = pl.BlockSpec((share, width), lambda i, s, b: (b[i], 0))
    row_out = pl.BlockSpec((share, width), lambda i, s, b: (i, 0))
    first = pl.BlockSpec((share, width), lambda i, s, b: (0, 0))
    line = pl.BlockSpec((1, width), lambda i, s, b: (0, 0))
    full = jax.ShapeDtypeStruct((rows, width), bf16)
    return pl.pallas_call(
        kernel,
        out_shape=(jax.ShapeDtypeStruct((share, width), bf16), full) if norm else full,
        grid_spec=pltpu.PrefetchScalarGridSpec(
            num_scalar_prefetch=2,
            grid=(blocks,),
            in_specs=[row_in, line, line] if norm else [row_in],
            out_specs=(first, row_out) if norm else row_out,
            scratch_shapes=[pltpu.VMEM((share, width), bf16)] if norm else [],
        ),
        compiler_params=params(24),
        cost_estimate=cost(10 * rows * width, 4 * rows * width),
    )(ring.slots, row_blocks, values, *((gain, shift) if norm else ()))


def slot_list(chunks, axis):
    if chunks[0].shape[axis] % 128 != 0:
        return [jnp.concatenate(chunks, axis=axis)]
    return chunks


def chunk_sum(left, chunks, turned, tile, extras, finish, outs, megabytes=40):
    chunks = slot_list(chunks, 1 if turned else 0)
    rows, depth = left.shape
    count = len(chunks)
    piece = depth // count
    columns = chunks[0].shape[0 if turned else 1]
    tile = min(tile, columns)

    def kernel(*refs):
        left_ref = refs[0]
        chunk_refs = refs[1 : 1 + count]
        extra_refs = refs[1 + count : 1 + count + len(extras)]
        out_refs = refs[1 + count + len(extras) :]
        step = min(rows, 256)
        for start in range(0, rows, step):
            at = slice(start, start + step)
            total = None
            for k in range(count):
                part = dot(
                    left_ref[at, k * piece : (k + 1) * piece],
                    chunk_refs[k][...],
                    NT if turned else NN,
                )
                total = part if total is None else total + part
            finish(total, extra_refs, out_refs, at)

    if turned:
        chunk_spec = pl.BlockSpec((tile, piece), lambda i: (i, 0))
    else:
        chunk_spec = pl.BlockSpec((piece, tile), lambda i: (0, i))
    return pl.pallas_call(
        kernel,
        out_shape=tuple(jax.ShapeDtypeStruct((r, columns), d) for d, r in outs),
        grid=(columns // tile,),
        in_specs=[pl.BlockSpec((rows, depth), lambda i: (0, 0))]
        + [chunk_spec] * count
        + [pl.BlockSpec((r, tile), lambda i: (0, i)) for _, r in extras],
        out_specs=tuple(pl.BlockSpec((r, tile), lambda i: (0, i)) for _, r in outs),
        compiler_params=params(megabytes),
        cost_estimate=cost(
            2 * rows * depth * columns, 2 * (rows * depth + depth * columns) + 8 * rows * columns
        ),
    )(left, *chunks, *(a for a, _ in extras))


def chunk_side(left, chunks, turned, megabytes=40):
    chunks = slot_list(chunks, 0 if turned else 1)
    rows, depth = left.shape
    count = len(chunks)
    piece = chunks[0].shape[0 if turned else 1]
    block = (piece, depth) if turned else (depth, piece)
    half = rows // 2

    def kernel(*refs):
        left_ref = refs[0]
        chunk_refs = refs[1 : 1 + count]
        keep_ref, send_ref, held, sems = refs[1 + count :]
        def copy(k):
            source = chunk_refs[k]
            if chunk_refs[k].shape != block:
                source = source.at[:, :depth] if turned else source.at[:depth, :]
            return pltpu.make_async_copy(source, held.at[k], sems.at[k])
        for k in range(count):
            copy(k).start()
        for k in range(count):
            copy(k).wait()
            for out_ref, start in ((keep_ref, 0), (send_ref, half)):
                part = dot(left_ref[start : start + half, :], held[k], NT if turned else NN)
                out_ref[:, k * piece : (k + 1) * piece] = part.astype(bf16)

    shape = jax.ShapeDtypeStruct((half, piece * count), bf16)
    return pl.pallas_call(
        kernel,
        out_shape=(shape, shape),
        in_specs=[pl.BlockSpec(memory_space=pltpu.VMEM)]
        + [pl.BlockSpec(memory_space=pl.ANY)] * count,
        out_specs=(pl.BlockSpec(memory_space=pltpu.VMEM),) * 2,
        scratch_shapes=[pltpu.VMEM((count,) + block, bf16), pltpu.SemaphoreType.DMA((count,))],
        compiler_params=params(megabytes),
        cost_estimate=cost(
            2 * rows * depth * piece * count,
            2 * (rows * depth + depth * piece * count + rows * piece * count),
        ),
    )(left, *chunks)


def mask_of(info_ref, key_ref, keys):
    own, one, two, place = (info_ref[i : i + 1, :] for i in range(4))
    seg = key_ref[keys, 0:1]
    spot = key_ref[keys, 1:2]
    return ((seg == own) | (seg == one) | (seg == two)) & (spot <= place)


def attend(qkv, kv_blocks, key_info, query_info, heads, head, scale, rows_at_once=512):
    rows = qkv.shape[0]
    count = len(kv_blocks)
    span = kv_blocks[0].shape[0]
    keys = span * count

    def kernel(q_ref, *refs):
        kv_refs = refs[:count]
        key_ref, info_ref, out_ref, log_ref, turned, score = refs[count:]

        @pl.when(pl.program_id(0) == 0)
        def _():
            for d in range(count):
                turned[:, d * span : (d + 1) * span] = kv_refs[d][:, head:].T

        masks = [
            mask_of(info_ref, key_ref, slice(d * span, (d + 1) * span)) for d in range(count)
        ]
        for h in range(heads):
            query = q_ref[:, h * head : (h + 1) * head]
            top = None
            for d in range(count):
                raw = dot(kv_refs[d][:, :head], query, NT)
                raw = jnp.where(masks[d], raw, masked_score / scale)
                score[d * span : (d + 1) * span, :] = raw
                peak = jnp.max(raw, axis=0, keepdims=True)
                top = peak if top is None else jnp.maximum(top, peak)
            total = mixed = None
            for d in range(count):
                e = jnp.exp2((score[d * span : (d + 1) * span, :] - top) * (scale * log2_e))
                summed = jnp.sum(e, axis=0, keepdims=True)
                total = summed if total is None else total + summed
                part = dot(turned[:, d * span : (d + 1) * span], e.astype(bf16), NN)
                mixed = part if mixed is None else mixed + part
            out_ref[:, h * head : (h + 1) * head] = (mixed * (1.0 / total)).T.astype(bf16)
            log_ref[h : h + 1, :] = (top * scale + jnp.log(total)) * log2_e

    block = min(rows_at_once, rows)
    return pl.pallas_call(
        kernel,
        out_shape=(
            jax.ShapeDtypeStruct((rows, heads * head), bf16),
            jax.ShapeDtypeStruct((8, rows), f32),
        ),
        grid=(rows // block,),
        in_specs=[pl.BlockSpec((block, heads * head), lambda i: (i, 0))]
        + [pl.BlockSpec((span, 2 * head), lambda i: (0, 0))] * count
        + [
            pl.BlockSpec((keys, 2), lambda i: (0, 0)),
            pl.BlockSpec((8, block), lambda i: (0, i)),
        ],
        out_specs=(
            pl.BlockSpec((block, heads * head), lambda i: (i, 0)),
            pl.BlockSpec((8, block), lambda i: (0, i)),
        ),
        scratch_shapes=[
            pltpu.VMEM((head, keys), bf16),
            pltpu.VMEM((keys, block), f32),
        ],
        compiler_params=params(40),
        cost_estimate=cost(4 * rows * keys * heads * head, 4 * rows * heads * head, rows * keys * heads),
    )(qkv, *kv_blocks, key_info, query_info)


def attend_back(qkv, kv_blocks, key_info, query_info, logs, grad, out, heads, head, scale, rows_at_once=256):
    rows = qkv.shape[0]
    count = len(kv_blocks)
    span = kv_blocks[0].shape[0]
    keys = span * count

    def kernel(q_ref, *refs):
        kv_refs = refs[:count]
        key_ref, info_ref, log_ref, grad_ref, out_ref, dq_ref, dkv_ref, turned = refs[count:]

        @pl.when(pl.program_id(0) == 0)
        def _():
            for d in range(count):
                turned[:, d * span : (d + 1) * span] = kv_refs[d][:, :head].T
            dkv_ref[...] = jnp.zeros_like(dkv_ref)

        masks = [
            mask_of(info_ref, key_ref, slice(d * span, (d + 1) * span)) for d in range(count)
        ]
        for h in range(heads):
            cols = slice(h * head, (h + 1) * head)
            query = q_ref[:, cols]
            pulled = grad_ref[:, cols]
            log = log_ref[h : h + 1, :]
            delta = jnp.sum(
                (pulled.astype(f32) * out_ref[:, cols].astype(f32)).T, axis=0, keepdims=True
            )
            mixed = None
            for d in range(count):
                at = slice(d * span, (d + 1) * span)
                raw = dot(kv_refs[d][:, :head], query, NT) * (scale * log2_e)
                p = jnp.exp2(jnp.where(masks[d], raw, masked_score) - log)
                g = dot(kv_refs[d][:, head:], pulled, NT)
                ds = (p * (g - delta)).astype(bf16)
                dkv_ref[at, head:] += dot(p.astype(bf16), pulled, NN)
                dkv_ref[at, :head] += dot(ds, query, NN) * scale
                part = dot(turned[:, at], ds, NN)
                mixed = part if mixed is None else mixed + part
            dq_ref[:, cols] = (mixed * scale).T.astype(bf16)

    block = min(rows_at_once, rows)
    return pl.pallas_call(
        kernel,
        out_shape=(
            jax.ShapeDtypeStruct((rows, heads * head), bf16),
            jax.ShapeDtypeStruct((keys, 2 * head), f32),
        ),
        grid=(rows // block,),
        in_specs=[pl.BlockSpec((block, heads * head), lambda i: (i, 0))]
        + [pl.BlockSpec((span, 2 * head), lambda i: (0, 0))] * count
        + [
            pl.BlockSpec((keys, 2), lambda i: (0, 0)),
            pl.BlockSpec((8, block), lambda i: (0, i)),
            pl.BlockSpec((8, block), lambda i: (0, i)),
            pl.BlockSpec((block, heads * head), lambda i: (i, 0)),
            pl.BlockSpec((block, heads * head), lambda i: (i, 0)),
        ],
        out_specs=(
            pl.BlockSpec((block, heads * head), lambda i: (i, 0)),
            pl.BlockSpec((keys, 2 * head), lambda i: (0, 0)),
        ),
        scratch_shapes=[
            pltpu.VMEM((head, keys), bf16),
        ],
        compiler_params=params(44),
        cost_estimate=cost(
            10 * rows * keys * heads * head, 8 * keys * head + 6 * rows * heads * head, rows * keys * heads
        ),
    )(qkv, *kv_blocks, key_info, query_info, logs, grad, out)


def parent_lookup(seg_ids, parents):
    labels = jnp.arange(parents.shape[0], dtype=jnp.int32)
    picked = jnp.where(seg_ids[:, None] == labels[None, :], parents[None, :], 0)
    return jnp.sum(picked, axis=1)


def gelu_parts(values):
    scale = math.sqrt(2.0 / math.pi)
    squared = values * values
    bend = jnp.tanh(scale * (values + 0.044715 * squared * values))
    out = 0.5 * values * (1.0 + bend)
    slope = 0.5 * (1.0 + bend) + 0.5 * values * (1.0 - bend * bend) * scale * (
        1.0 + 3 * 0.044715 * squared
    )
    return out, slope


def body(
    tokens,
    token_segment,
    segment_parent,
    ln1_gain,
    ln1_bias,
    q_weight,
    q_bias,
    kv_weight,
    value_bias,
    o_weight,
    o_bias,
    ln2_gain,
    ln2_bias,
    up_weight,
    up_bias,
    down_weight,
    down_bias,
    out_grad,
):
    row_count, width = tokens.shape
    head_size = value_bias.shape[0]
    local_width = q_weight.shape[1]
    local_heads = local_width // head_size
    tree_length = token_segment.shape[0]
    score_scale = 1.0 / math.sqrt(head_size)
    ctx_count = lax.axis_size("ctx")
    tp_count = lax.axis_size("tp")
    ctx_index = lax.axis_index("ctx")
    tp_index = lax.axis_index("tp")
    share_rows = row_count // tp_count
    ring = Ring(lax.axis_size("fsdp"), ctx_count, lax.axis_index("fsdp") * ctx_count + ctx_index)
    n = ring.size
    piece = width // n

    qkv_slots = ring.gather(jnp.concatenate([q_weight, kv_weight], axis=1), True)
    o_slots = ring.gather(o_weight, False)
    half = n // 2
    up_slots = ring.gather(up_weight, False, o_slots[1], o_slots[n - 1])
    down_slots = ring.gather(down_weight, True, up_slots[1], up_slots[n - 1])

    masks = [0]
    for bit in reversed(list(bits_of("tp"))):
        masks = masks + [m ^ bit for m in masks]
    row_blocks = [tp_index ^ m for m in masks]

    def rows_in(values):
        return jnp.concatenate(
            [
                lax.dynamic_slice_in_dim(values, b * share_rows, share_rows, 0)
                for b in row_blocks
            ],
            axis=0,
        )

    row_ids = jnp.stack(row_blocks)
    x_low_share, act_one = arrange(
        tokens, ln1_gain.astype(f32)[None], ln1_bias.astype(f32)[None], ring, row_ids
    )
    g_low = arrange(out_grad, None, None, ring, row_ids)
    vectors = ring.into(
        jnp.stack([ln1_gain, ln1_bias, o_bias, ln2_gain, ln2_bias, down_bias]).astype(f32)
    )
    gain_one, _, o_shift, gain_two, shift_two, down_shift = (
        vectors[i : i + 1] for i in range(6)
    )
    own_place = rows_in(jnp.arange(row_count, dtype=jnp.int32))

    parents = segment_parent[0]
    query_place = ctx_index * row_count + own_place
    key_places = []
    for d in range(ctx_count):
        start = (ctx_index - d) * row_count
        key_places.append(jnp.where(start >= 0, start + own_place, tree_length))
    key_place = jnp.concatenate(key_places)
    segment_blocks = rows_in(token_segment.reshape(ctx_count, row_count).T)
    own_seg = lax.dynamic_slice_in_dim(segment_blocks, ctx_index, 1, 1)[:, 0]
    key_segment = jnp.concatenate(
        [
            lax.dynamic_slice_in_dim(
                segment_blocks, lax.rem(ctx_index - d + ctx_count, ctx_count), 1, 1
            )[:, 0]
            for d in range(ctx_count)
        ]
    )
    seg_one = parent_lookup(own_seg, parents)
    seg_two = parent_lookup(seg_one, parents)
    key_info = jnp.stack([key_segment, key_place], axis=1)
    blank = jnp.zeros_like(own_seg)
    query_info = jnp.stack([own_seg, seg_one, seg_two, query_place, blank, blank, blank, blank])

    qkv_shift = jnp.concatenate(
        [q_bias.astype(f32), jnp.zeros((head_size,), f32), value_bias.astype(f32)]
    )

    def add_shift(total, extra, out, at):
        out[0][at, :] = (total + extra[0][...]).astype(bf16)

    (qkv,) = chunk_sum(
        act_one, qkv_slots, False, 256, [(qkv_shift[None], 1)], add_shift, [(bf16, row_count)]
    )
    kv_own = qkv[:, local_width:]
    kv_blocks = [kv_own] + [
        lax.ppermute(kv_own, "ctx", [(c, c + d) for c in range(ctx_count - d)])
        for d in range(1, ctx_count)
    ]
    attended, logs = attend(
        qkv, kv_blocks, key_info, query_info, local_heads, head_size, score_scale
    )
    attn_share = share_sum(*chunk_side(attended, o_slots, False))
    x_share = x_low_share.astype(f32)
    residual = x_share + (attn_share + o_shift)
    norm_two, inv_two = normed(residual)
    act_two = share_spread((norm_two * gain_two + shift_two).astype(bf16))


    def activate(total, extra, out, at):
        gelu_out, gelu_slope = gelu_parts(total + extra[0][...])
        out[0][at, :] = gelu_out.astype(bf16)
        out[1][at, :] = gelu_slope

    hidden, gelu_slope = chunk_sum(
        act_two,
        up_slots,
        False,
        512,
        [(up_bias.astype(f32)[None], 1)],
        activate,
        [(bf16, row_count), (f32, row_count)],
    )
    down_w_grad = ring.scatter(
        lambda k: dot(hidden, g_low[:, k * piece : (k + 1) * piece], TN), False
    )

    def deactivate(total, extra, out, at):
        low = (total * extra[0][at, :]).astype(bf16)
        out[0][at, :] = low
        summed = jnp.sum(low.astype(f32), axis=0, keepdims=True)
        out[1][...] = summed if at.start == 0 else out[1][...] + summed

    grad_pre, up_bias_grad = chunk_sum(
        g_low,
        down_slots,
        True,
        512,
        [(gelu_slope, row_count)],
        deactivate,
        [(bf16, row_count), (f32, 1)],
    )
    up_bias_grad = up_bias_grad[0]
    up_w_grad = ring.scatter(
        lambda k: dot(act_two[:, k * piece : (k + 1) * piece], grad_pre, TN), True
    )
    grad_two = share_sum(*chunk_side(grad_pre, up_slots, True))

    g_share = g_low[:share_rows].astype(f32)
    grad_res = g_share + normed_back(grad_two, gain_two, norm_two, inv_two)
    grad_attn_share = grad_res.astype(bf16)
    grad_attn = share_spread(grad_attn_share)
    out_w_grad, out_resume = ring.scatter(
        lambda k: dot(attended, grad_attn[:, k * piece : (k + 1) * piece], TN), False, 1
    )

    def only_round(total, extra, out, at):
        out[0][at, :] = total.astype(bf16)

    (grad_attended,) = chunk_sum(
        grad_attn, o_slots, True, 256, [], only_round, [(bf16, row_count)]
    )
    ffn_share = share_sum(*chunk_side(after(hidden, grad_attended), down_slots, False))
    layer_out = ring.back((residual + (ffn_share + down_shift)).astype(bf16))
    early = jnp.stack(
        [
            jnp.sum(g_share, axis=0),
            jnp.sum(grad_attn_share.astype(f32), axis=0),
            jnp.sum(grad_two * norm_two, axis=0),
            jnp.sum(grad_two, axis=0),
        ]
    )
    early = ring.back(early).reshape(-1)

    grad_query, kv_grad = attend_back(
        qkv, kv_blocks, key_info, query_info, logs, grad_attended, attended,
        local_heads, head_size, score_scale,
    )
    q_bias_grad = jnp.sum(grad_query.astype(f32), axis=0)

    kv_part = kv_grad.astype(bf16).reshape(ctx_count, 2, row_count // 2, 2 * head_size)
    kv_part = share_sum(
        kv_part[:, 0].reshape(-1, 2 * head_size),
        kv_part[:, 1].reshape(-1, 2 * head_size),
        ctx_count,
    ).reshape(ctx_count, share_rows, 2 * head_size)
    kv_sum = kv_part[0]
    for d in range(1, ctx_count):
        kv_sum = kv_sum + lax.ppermute(
            kv_part[d].astype(bf16), "ctx", [(c, c - d) for c in range(d, ctx_count)]
        ).astype(f32)
    kv_low_share = kv_sum.astype(bf16)
    kv_low = share_spread(kv_low_share)
    out_resume(kv_low_share)

    sub = piece // tp_count

    def q_kv_part(k):
        act_piece = act_one[:, k * piece : (k + 1) * piece]
        q_piece = dot(act_piece, grad_query, TN)
        kv_piece = lax.dynamic_slice_in_dim(dot(act_piece, kv_low, TN), tp_index * sub, sub, 0)
        kv_piece = jnp.concatenate([kv_piece[: sub // 2], kv_piece[sub // 2 :]], axis=1)
        return jnp.concatenate([q_piece, kv_piece], axis=0)

    q_kv = ring.scatter(q_kv_part, True)()
    q_w_grad = q_kv[:piece]
    kv_w_grad = jnp.concatenate(
        [q_kv[piece:, : 2 * head_size], q_kv[piece:, 2 * head_size :]], axis=0
    )

    kv_full = jnp.concatenate([c[:, local_width:] for c in qkv_slots], axis=0)
    grad_act = share_sum(*chunk_side(grad_query, qkv_slots, True)) + dot(
        kv_low_share, kv_full, NT
    )
    norm_share, inv_share = normed(x_share)
    input_grad = ring.back(
        (grad_res + normed_back(grad_act, gain_one, norm_share, inv_share)).astype(bf16)
    )
    late = jnp.stack([jnp.sum(grad_act * norm_share, axis=0), jnp.sum(grad_act, axis=0)])
    late = ring.back(late).reshape(-1)
    value_bias_grad = jnp.sum(kv_low_share[:, head_size:].astype(f32), axis=0)
    late = everyone_sum(jnp.concatenate([late, value_bias_grad, early]), ("tp",))
    early = late[2 * width + head_size :]
    late = late[: 2 * width + head_size]
    sums = [late, early, q_bias_grad, up_bias_grad]
    cuts = np.cumsum([v.shape[0] for v in sums])
    sums = everyone_sum(jnp.concatenate(sums), ("ctx", "fsdp"))
    late, early, q_bias_out, up_bias_out = (
        sums[stop - v.shape[0] : stop]
        for stop, v in zip(cuts, (late, early, q_bias_grad, up_bias_grad))
    )
    early = early.reshape(4, width)
    down_w_grad = down_w_grad(grad_query)
    up_w_grad = up_w_grad(grad_query)
    out_w_grad = out_w_grad(None)
    return (
        layer_out,
        input_grad,
        late[:width],
        late[width : 2 * width],
        q_w_grad,
        q_bias_out,
        kv_w_grad,
        late[2 * width :],
        out_w_grad,
        early[1],
        early[2],
        early[3],
        up_w_grad,
        up_bias_out,
        down_w_grad,
        early[0],
    )


def solution(mesh):
    whole = P()
    rows = P(("fsdp", "ctx"), None)
    split = P(("fsdp", "ctx"), "tp")
    turned = P("tp", ("fsdp", "ctx"))
    thin = P(("fsdp", "ctx", "tp"), None)
    in_specs = (
        rows, P("fsdp"), P("fsdp", None), whole, whole, split, P("tp"), rows, whole,
        turned, whole, whole, whole, split, P("tp"), turned, whole, rows,
    )
    out_specs = (
        thin, thin, whole, whole, split, P("tp"), thin, whole, turned, whole, whole, whole,
        split, P("tp"), turned, whole,
    )
    return jax.shard_map(body, mesh=mesh, in_specs=in_specs, out_specs=out_specs, check_vma=False)
```
